32 devices in a mesh: dp: 8 (over z, y), tensor: 4 (over x, core).
Axes of the slice: x: 2, y: 2, z: 4, core: 2. Of those that a mesh axis runs over, the one named last changes fastest.
Arguments:
- queries: bfloat16 [7168, 4096], P('dp', 'tensor'), may hold values from -40 to 40
- passages: bfloat16 [7168, 4096], P('dp', 'tensor'), may hold values from -40 to 40
- matching: int32 [56, 8], P('dp'), may hold values from 0 to 55, as said below
Outputs:
- grad_queries: bfloat16 [7168, 4096], P('dp', 'tensor')
- grad_passages: bfloat16 [7168, 4096], P('dp', 'tensor')
- loss: float32 [], replicated
The draws below stay inside these ranges and needn't reach their ends.
Inputs may be any that keep to these rules, and one draw needn't show every extreme that they name: The 56 entries of matching on one dp index name clusters of any one dp index at most 7 times, and some dp index exactly 7 times.
All inputs are finite; a program needn't handle non-finite values.
Results may differ from the reference program's by a relative error of at most 0.0038.
Values may be sent and summed in bfloat16 or wider, within the bound.
No kernel may reach another device: no remote copies, remote signals or barrier semaphores. Data moves between devices by JAX's collectives and lax.ppermute only.
A program may use at most 128 MiB of HBM per device.

```python
import jax
import jax.numpy as jnp
from jax import lax

D = 4096
CLUSTER = 128
PARTNERS = 8
CL_DEV = 7
NCL = 56


def embed_pair(key):
    base_key = jax.random.fold_in(key, 11)
    key_query, key_passage = jax.random.split(base_key, 2)
    total_rows = NCL * CLUSTER
    query_raw = jnp.clip(jax.random.normal(key_query, (total_rows, D), jnp.float32), -4.0, 4.0)
    passage_raw = jnp.clip(jax.random.normal(key_passage, (total_rows, D), jnp.float32), -4.0, 4.0)
    cluster_pos = (jnp.arange(total_rows) // CLUSTER).astype(jnp.float32)[:, None]
    rise_factor = 1.0 + cluster_pos / max(NCL - 1, 1)
    passage_out = passage_raw * rise_factor
    query_out = query_raw * rise_factor
    return (query_out, passage_out)


def draw_queries(key, part):
    return embed_pair(key)[0].astype(jnp.bfloat16)


def draw_passages(key, part):
    return embed_pair(key)[1].astype(jnp.bfloat16)


def draw_matching(key, part):
    device_count = NCL // CL_DEV
    request_count = CL_DEV * PARTNERS
    base_key = jax.random.fold_in(key, 23)

    def one_device(device_key):
        key_owner, key_order, key_local = jax.random.split(device_key, 3)
        owner_perm = jax.random.permutation(key_owner, device_count)
        order_perm = jax.random.permutation(key_order, request_count)
        owner_ids = owner_perm[order_perm % device_count]
        local_ids = jax.random.randint(key_local, (request_count,), 0, CL_DEV)
        return (owner_ids * CL_DEV + local_ids).reshape(CL_DEV, PARTNERS)
    result = jax.vmap(one_device)(jax.random.split(base_key, device_count))
    return result.reshape(NCL, PARTNERS).astype(jnp.int32)


def setup_inputs(seed: int = 0) -> dict:
    key_of = jax.random.split(jax.random.key(seed), 4)
    return {
        "queries": draw_queries(jax.random.fold_in(key_of[3], 71), 0),
        "passages": draw_passages(jax.random.fold_in(key_of[3], 71), 0),
        "matching": draw_matching(jax.random.fold_in(key_of[3], 71), 0),
    }


def reference(queries, passages, matching):
    clusters = matching.shape[0]
    features = queries.shape[1]
    query_block = queries.reshape(clusters, CLUSTER, features)
    passage_block = passages.reshape(clusters, CLUSTER, features)
    key_table = jnp.concatenate([jnp.arange(clusters, dtype=jnp.int32)[:, None], matching.astype(jnp.int32)], axis=1)
    blocks = PARTNERS + 1
    target = (jnp.arange(CLUSTER)[:, None] == jnp.arange(blocks * CLUSTER)[None, :]).astype(jnp.float32)
    score_scale = features ** (-0.5)

    def visit(cluster_at, carry):
        grad_q, grad_p, loss_total = carry
        key_ids = key_table[cluster_at]
        key_rows = jnp.take(passage_block, key_ids, axis=0).reshape(blocks * CLUSTER, features)
        query_rows = query_block[cluster_at]
        logits = jnp.dot(query_rows, key_rows.T, preferred_element_type=jnp.float32) * score_scale
        row_max = lax.optimization_barrier(jnp.max(logits, axis=-1, keepdims=True))
        log_total = row_max + jnp.log(lax.optimization_barrier(jnp.sum(jnp.exp(logits - row_max), axis=-1, keepdims=True)))
        chances = jnp.exp(logits - log_total)
        cross_ent = log_total[:, 0] - lax.optimization_barrier(jnp.sum(logits * target, axis=-1))
        weights = (chances - target).astype(jnp.bfloat16)
        grad_q = grad_q.at[cluster_at].set(jnp.dot(weights, key_rows, preferred_element_type=jnp.float32))
        contrib = jnp.dot(weights.T, query_rows, preferred_element_type=jnp.float32).reshape(blocks, CLUSTER, features)
        others = lax.optimization_barrier(contrib[1:].astype(jnp.bfloat16)).astype(jnp.float32)
        contrib = jnp.concatenate([contrib[:1], others], axis=0)
        grad_p = grad_p.at[key_ids].add(contrib)
        return (grad_q, grad_p, loss_total + jnp.sum(cross_ent))
    start = (jnp.zeros((clusters, CLUSTER, features), jnp.float32), jnp.zeros((clusters, CLUSTER, features), jnp.float32), jnp.zeros((), jnp.float32))
    grad_q, grad_p, loss_total = lax.fori_loop(0, clusters, visit, start)
    total = jnp.sum(grad_q * grad_q) + jnp.sum(grad_p * grad_p)
    all_rows = clusters * CLUSTER
    clip_limit = 0.25 * jnp.sqrt(jnp.float32(2 * all_rows * features))
    factor = jnp.minimum(jnp.float32(1.0), clip_limit / jnp.sqrt(total + 1e-06))
    grad_queries = (grad_q * factor).astype(jnp.bfloat16).reshape(all_rows, features)
    grad_passages = (grad_p * factor).astype(jnp.bfloat16).reshape(all_rows, features)
    return (grad_queries, grad_passages, loss_total / all_rows)
```

```python
import functools

import jax
import jax.numpy as jnp
from jax import lax
from jax.experimental import pallas as pl
from jax.experimental.pallas import tpu as pltpu
from jax.sharding import PartitionSpec as P

CLUSTER = 128
PARTNERS = 8
LOW = -3.0e38
VALID = 1 << 16
VMEM_LIMIT = 56 * 1024 * 1024

VM = pl.BlockSpec(memory_space=pltpu.VMEM)
SM = pl.BlockSpec(memory_space=pltpu.SMEM)
NT = (((1,), (1,)), ((), ()))
TN = (((0,), (0,)), ((), ()))
NN = (((1,), (0,)), ((), ()))


def bits_of(size):
    return size.bit_length() - 1


def swap(value, axis, mask):
    size = lax.axis_size(axis)
    return lax.ppermute(value, axis, [(i, i ^ mask) for i in range(size)])


def call(kernel, out_shape, scratch, flops, moved, args, smem):
    return pl.pallas_call(
        kernel,
        out_shape=out_shape,
        in_specs=[SM] * smem + [VM] * (len(args) - smem),
        out_specs=jax.tree.map(lambda _: VM, out_shape),
        scratch_shapes=scratch,
        compiler_params=pltpu.CompilerParams(vmem_limit_bytes=VMEM_LIMIT),
        cost_estimate=pl.CostEstimate(flops=flops, bytes_accessed=moved, transcendentals=0),
    )(*args)


def unpack(code):
    return code >= VALID, (code >> 8) & 255, code & 255


def groups_of(mask, clusters, cap):
    base = clusters if mask == 0 else 0
    return [(0, base), (1, base + cap)]


def logits_kernel(mask, clusters, cap, ways, tab, rank, mine, other, keys, low, high, block):
    share = CLUSTER // ways
    me = rank[0]

    def one(rows, key, slot):
        block[...] = lax.dot_general(rows, key, NT, preferred_element_type=jnp.float32)
        for at in range(ways):
            start = pl.multiple_of((me ^ at) * share, share)
            (high if at % 2 else low)[at // 2, slot] = block[pl.ds(start, share), :]

    if mask == 0:

        @pl.loop(0, clusters)
        def _(c):
            one(mine[c], keys[c], c)

    for requester, first in groups_of(mask, clusters, cap):
        rows_ref = other if requester else mine

        @pl.loop(0, cap)
        def _(j):
            _, c, e = unpack(tab[requester, mask * cap + j])
            one(rows_ref[c], keys[e], first + j)


def each_slot(visit, chunks, clusters, cap, tab):
    for mask, ref in enumerate(chunks):
        if mask == 0:
            for c in range(clusters):
                visit(mask, ref, c, c, None)
        for requester, first in groups_of(mask, clusters, cap):

            @pl.loop(0, cap)
            def _(j):
                ok, c, _ = unpack(tab[requester, mask * cap + j])
                at = jnp.where(ok, requester * clusters + c, 2 * clusters)
                visit(mask, ref, first + j, at, ok)


def stats_kernel(parts, clusters, cap, scale, tab, *refs):
    chunks, stats, top, total = refs[:parts], refs[parts], refs[parts + 1], refs[parts + 2]
    top[...] = jnp.full_like(top, LOW)
    total[...] = jnp.zeros_like(total)

    def raise_top(mask, ref, slot, at, ok):
        top[at] = jnp.maximum(top[at], ref[slot] * scale)

    each_slot(raise_top, chunks, clusters, cap, tab)
    for c in range(2 * clusters + 1):
        top[c] = jnp.broadcast_to(jnp.max(top[c], axis=-1, keepdims=True), top.shape[1:])

    def add_total(mask, ref, slot, at, ok):
        total[at] = total[at] + jnp.exp(ref[slot] * scale - top[at])

    each_slot(add_total, chunks, clusters, cap, tab)
    lane = lax.broadcasted_iota(jnp.int32, stats.shape, 1)
    out = jnp.zeros(stats.shape, jnp.float32)
    for c in range(2 * clusters):
        out = jnp.where(lane == c, top[c], out)
        sums = jnp.sum(total[c], axis=-1, keepdims=True)
        out = jnp.where(lane == 2 * clusters + c, sums, out)
    stats[...] = out


def weights_kernel(parts, clusters, cap, scale, tab, rank, *refs):
    chunks, here, there = refs[:parts], refs[parts], refs[parts + 1]
    outs, loss, level = refs[parts + 2 : 2 * parts + 2], refs[2 * parts + 2], refs[2 * parts + 3]
    shape = here.shape
    row = lax.broadcasted_iota(jnp.int32, shape, 0) + rank[0] * shape[0]
    lane = lax.broadcasted_iota(jnp.int32, shape, 1)
    target = (row == lane).astype(jnp.float32)
    for c in range(2 * clusters):
        p = (c + clusters) % (2 * clusters)
        top_a, top_b = here[:, c : c + 1], there[:, p : p + 1]
        k = 2 * clusters
        sum_a, sum_b = here[:, k + c : k + c + 1], there[:, k + p : k + p + 1]
        top = jnp.maximum(top_a, top_b)
        total = sum_a * jnp.exp(top_a - top) + sum_b * jnp.exp(top_b - top)
        level[c] = jnp.broadcast_to(top + jnp.log(total), shape)
    level[2 * clusters] = jnp.zeros(shape, jnp.float32)
    loss[...] = jnp.zeros(shape, jnp.float32)

    def weigh(mask, ref, slot, at, ok):
        logits = ref[slot] * scale
        chances = jnp.exp(logits - level[at])
        if ok is None:
            chances = chances - target
            loss[...] += jnp.where(lane == 0, level[at], 0.0) - logits * target
        else:
            chances = jnp.where(ok, chances, 0.0)
        outs[mask][slot] = chances.astype(jnp.bfloat16)

    each_slot(weigh, chunks, clusters, cap, tab)


def whole_weights(pieces, order, me, slot, wide):
    share = CLUSTER // len(order)
    for piece, at in zip(pieces, order):
        start = pl.multiple_of((me ^ at) * share, share)
        wide[pl.ds(start, share), :] = piece[slot]
    return wide[...]


def term_kernel(mask, clusters, cap, order, arrived, tab, rank, mine, other, *refs):
    ways = len(order)
    pieces, came, out = refs[:ways], refs[ways : ways + arrived], refs[ways + arrived]
    wide, total = refs[ways + arrived + 1 :]
    me = rank[0]
    if mask == 0:

        @pl.loop(0, clusters)
        def _(c):
            w = whole_weights(pieces, order, me, c, wide)
            total[c] = lax.dot_general(w, mine[c], TN, preferred_element_type=jnp.float32)

    else:
        total[...] = jnp.zeros_like(total)
    for requester, first in groups_of(mask, clusters, cap):
        rows_ref = other if requester else mine

        @pl.loop(0, cap)
        def _(j):
            _, c, e = unpack(tab[requester, mask * cap + j])
            w = whole_weights(pieces, order, me, first + j, wide)
            total[e] += lax.dot_general(w, rows_ref[c], TN, preferred_element_type=jnp.float32)

    @pl.loop(0, clusters)
    def _(c):
        value = total[c]
        for ref in came:
            value = value + ref[c].astype(jnp.float32)
        out[c] = value.astype(out.dtype)


def query_kernel(requester, parts, clusters, cap, order, tab, rank, *refs):
    ways = len(order)
    keys = refs[:parts]
    pieces = [refs[parts + m * ways : parts + (m + 1) * ways] for m in range(parts)]
    out, wide, total = refs[parts + parts * ways :]
    me = rank[0]
    if requester == 0:

        @pl.loop(0, clusters)
        def _(c):
            w = whole_weights(pieces[0], order, me, c, wide)
            total[c] = lax.dot_general(w, keys[0][c], NN, preferred_element_type=jnp.float32)

    else:
        total[...] = jnp.zeros_like(total)
    for mask in range(parts):
        first = groups_of(mask, clusters, cap)[requester][1]

        @pl.loop(0, cap)
        def _(j):
            _, c, e = unpack(tab[requester, mask * cap + j])
            w = whole_weights(pieces[mask], order, me, first + j, wide)
            total[c] += lax.dot_general(w, keys[mask][e], NN, preferred_element_type=jnp.float32)

    @pl.loop(0, clusters)
    def _(c):
        out[c] = total[c].astype(out.dtype)


def shards(queries, passages, matching):
    bf16, f32 = jnp.bfloat16, jnp.float32
    size, ways = lax.axis_size("dp"), lax.axis_size("tensor")
    clusters, width = matching.shape[0], queries.shape[1]
    requests = clusters * PARTNERS
    cap = -(-requests // size)
    parts = size // 2
    share = CLUSTER // ways
    scale = (width * ways) ** (-0.5)
    cube = (clusters, CLUSTER, width)
    mine, own_keys = queries.reshape(cube), passages.reshape(cube)
    here = lax.axis_index("dp").astype(jnp.int32)
    rank = lax.axis_index("tensor").astype(jnp.int32).reshape(1)

    held = {0: own_keys}
    for bit in reversed(range(bits_of(parts))):
        for mask in sorted(held):
            held[mask | (1 << bit)] = swap(held[mask], "dp", 1 << bit)
    keys = [held[m] for m in range(parts)]
    both = jnp.stack([matching, swap(matching, "dp", parts)]).reshape(2, requests)
    other = swap(mine, "dp", parts)

    owner, local = both // clusters, both % clusters
    earlier = jnp.arange(requests)[None, :] < jnp.arange(requests)[:, None]
    same = owner[:, :, None] == owner[:, None, :]
    place = (owner ^ here) * cap + jnp.sum(jnp.where(same & earlier[None], 1, 0), axis=2)
    asker = (jnp.arange(requests) // PARTNERS)[None, :]
    code = VALID + asker * 256 + local
    slots = jnp.arange(parts * cap)[None, :, None] == place[:, None, :]
    tab = jnp.sum(jnp.where(slots, code[:, None, :], 0), axis=2).astype(jnp.int32)

    count = [2 * cap + (clusters if m == 0 else 0) for m in range(parts)]
    unit = 2 * CLUSTER * CLUSTER * width
    block_bytes = CLUSTER * width * 2
    chunks = []
    for m in range(parts):
        half = jax.ShapeDtypeStruct((ways // 2, count[m], share, CLUSTER), f32)
        keep, give = call(
            functools.partial(logits_kernel, m, clusters, cap, ways),
            (half, half),
            [pltpu.VMEM((CLUSTER, CLUSTER), f32)],
            count[m] * unit,
            3 * clusters * block_bytes,
            (tab, rank, mine, other, keys[m]),
            2,
        )
        got = swap(give, "tensor", 1)
        bit = 1
        while (1 << bit) < ways:
            keep = keep + got
            pairs = keep.reshape((keep.shape[0] // 2, 2) + keep.shape[1:])
            keep = pairs[:, 0]
            got = swap(pairs[:, 1], "tensor", 1 << bit)
            bit += 1
        chunks.append((keep + got)[0])

    tile = jax.ShapeDtypeStruct((share, CLUSTER), f32)
    levels = pltpu.VMEM((2 * clusters + 1, share, CLUSTER), f32)
    stats = call(
        functools.partial(stats_kernel, parts, clusters, cap, scale),
        tile, [levels, levels], 0, 2 << 20, (tab, *chunks), 1,
    )
    facing = swap(stats, "dp", parts)
    *weights, loss_rows = call(
        functools.partial(weights_kernel, parts, clusters, cap, scale),
        [jax.ShapeDtypeStruct(c.shape, bf16) for c in chunks] + [tile],
        [levels], 0, 2 << 20, (tab, rank, *chunks, stats, facing), 2,
    )
    order = [0]
    for bit in reversed(range(bits_of(ways))):
        order += [at | (1 << bit) for at in order]
    pieces = []
    for m in range(parts):
        group = [weights[m]]
        for bit in reversed(range(bits_of(ways))):
            group += [swap(piece, "tensor", 1 << bit) for piece in group]
        pieces.append(group)

    grow = [pltpu.VMEM((CLUSTER, CLUSTER), bf16), pltpu.VMEM(cube, f32)]
    terms, came = {}, {}
    for m in sorted(range(parts), key=lambda m: (bin(m)[::-1].find("1") if m else 99, -m)):
        low = bits_of(m & -m) if m else bits_of(parts)
        came = [swap(terms[m | (1 << b)], "dp", 1 << b) for b in range(low)]
        add = came if m else []
        terms[m] = call(
            functools.partial(term_kernel, m, clusters, cap, order, len(add)),
            jax.ShapeDtypeStruct(cube, bf16 if m else f32),
            grow, count[m] * unit, 4 * clusters * block_bytes,
            (tab, rank, mine, other, *pieces[m], *add), 2,
        )
    grads = {}
    for requester in (1, 0):
        grads[requester] = call(
            functools.partial(query_kernel, requester, parts, clusters, cap, order),
            jax.ShapeDtypeStruct(cube, bf16 if requester else f32),
            grow, parts * cap * unit, (parts + 2) * clusters * block_bytes,
            (tab, rank, *keys, *[p for group in pieces for p in group]), 2,
        )
    grad_q = grads[0] + swap(grads[1], "dp", parts).astype(f32)
    grad_p = terms[0]
    for part in came:
        grad_p = grad_p + part.astype(f32)

    squares = jnp.sum(grad_q * grad_q) + jnp.sum(grad_p * grad_p)
    sums = jnp.stack([jnp.sum(loss_rows), squares])
    for bit in range(bits_of(ways)):
        sums = sums + swap(sums, "tensor", 1 << bit)
    for bit in range(bits_of(size)):
        sums = sums + swap(sums, "dp", 1 << bit)
    all_rows = clusters * CLUSTER * size
    clip_limit = 0.25 * jnp.sqrt(jnp.float32(2 * all_rows * width * ways))
    factor = jnp.minimum(jnp.float32(1.0), clip_limit / jnp.sqrt(sums[1] + 1e-06))
    flat = queries.shape
    grad_queries = (grad_q * factor).astype(bf16).reshape(flat)
    grad_passages = (grad_p * factor).astype(bf16).reshape(flat)
    return (grad_queries, grad_passages, sums[0] / all_rows)


def solution(mesh):
    in_specs = (P("dp", "tensor"), P("dp", "tensor"), P("dp", None))
    out_specs = (P("dp", "tensor"), P("dp", "tensor"), P())
    return jax.shard_map(shards, mesh=mesh, in_specs=in_specs, out_specs=out_specs, check_vma=False)
```

```python
import functools

import jax
import jax.numpy as jnp
from jax import lax
from jax.experimental import pallas as pl
from jax.experimental.pallas import tpu as pltpu
from jax.sharding import PartitionSpec as P

CLUSTER = 128
PARTNERS = 8
LOW = -3.0e38
VALID = 1 << 16
VMEM_LIMIT = 56 * 1024 * 1024
SLACK = 4 * 1024 * 1024
COST = 1000

VM = pl.BlockSpec(memory_space=pltpu.VMEM)
SM = pl.BlockSpec(memory_space=pltpu.SMEM)
ANY = pl.BlockSpec(memory_space=pl.ANY)
NT = (((1,), (1,)), ((), ()))
TN = (((0,), (0,)), ((), ()))
NN = (((1,), (0,)), ((), ()))


def bits_of(size):
    return size.bit_length() - 1


def swap(value, axis, mask):
    size = lax.axis_size(axis)
    return lax.ppermute(value, axis, [(i, i ^ mask) for i in range(size)])


def size_of(shape):
    return shape.size * shape.dtype.itemsize


def call(name, kernel, out_shape, scratch, flops, args, smem, waits=()):
    outs = jax.tree.leaves(out_shape)
    moved = sum(size_of(a) for a in args[smem:]) + sum(size_of(o) for o in outs)
    held = moved + sum(size_of(jax.ShapeDtypeStruct(x.shape, x.dtype)) for x in scratch)

    def body(*refs):
        kernel(*refs[: len(args)], *refs[len(args) + len(waits) :])

    return pl.pallas_call(
        body,
        name=name,
        out_shape=out_shape,
        in_specs=[SM] * smem + [VM] * (len(args) - smem) + [ANY] * len(waits),
        out_specs=jax.tree.map(lambda _: VM, out_shape),
        scratch_shapes=scratch,
        compiler_params=pltpu.CompilerParams(vmem_limit_bytes=min(held + SLACK, VMEM_LIMIT)),
        cost_estimate=pl.CostEstimate(flops=flops // COST, bytes_accessed=moved // COST, transcendentals=0),
    )(*args, *waits)


def unpack(code):
    return code >= VALID, (code >> 8) & 255, code & 255


def layout(parts, clusters, cap):
    plans = [
        [(m, 0) for m in range(min(parts, 2))],
        [(m, 1) for m in range(min(parts, 2))] + [(2, r) for r in (0, 1) if parts > 2],
        [(m, r) for m in range(3, parts) for r in (0, 1)],
    ]
    chunks = []
    for plan in plans:
        groups, first = [], clusters if (0, 0) in plan else 0
        for mask, requester in plan:
            groups.append((mask, requester, first))
            first += cap
        if groups:
            chunks.append((tuple(groups), first))
    return tuple(chunks)


def share_rows(me, at, share):
    return pl.ds(pl.multiple_of((me ^ at) * share, share), share)


def rows_of(ref, c, me, ways, cut=slice(None)):
    share = CLUSTER // ways
    blocks = [ref[c, share_rows(me, at, share), cut] for at in range(ways)]
    return jnp.concatenate(blocks, axis=0)


def logits_kernel(groups, splits, clusters, cap, ways, tab_a, tab_b, rank, *refs):
    tab = (tab_a, tab_b)
    share = CLUSTER // ways
    me = rank[0]
    askers = sorted({r for _, r, _ in groups})
    rows = dict(zip(askers, refs))
    at_ref, keys = len(askers), {}
    for m, split in splits:
        keys[m] = refs[at_ref : at_ref + split]
        at_ref += split
    low, high, done = refs[at_ref:]
    done[...] = jnp.zeros_like(done)

    def one(row_ref, c, mask, e, slot):
        row = rows_of(row_ref, c, me, ways)
        wide = keys[mask][0].shape[-1]
        block = None
        for i, key in enumerate(keys[mask]):
            part = lax.dot_general(
                row[:, i * wide : (i + 1) * wide], key[e], NT, preferred_element_type=jnp.float32
            )
            block = part if block is None else block + part
        for at in range(ways):
            (high if at % 2 else low)[at // 2, slot] = block[at * share : (at + 1) * share]

    if any(first and (mask, r) == (0, 0) for mask, r, first in groups):

        @pl.loop(0, clusters)
        def _(c):
            one(rows[0], c, 0, c, c)

    @pl.loop(0, cap)
    def _(j):
        for mask, requester, first in groups:
            _, c, e = unpack(tab[requester][mask * cap + j])
            one(rows[requester], c, mask, e, first + j)


def each_slot(visit, chunks, plans, clusters, cap, tab):
    for n, (groups, _) in enumerate(plans):
        if any(first and (mask, r) == (0, 0) for mask, r, first in groups):
            for c in range(clusters):
                visit(n, chunks[n], c, c, None)

        @pl.loop(0, cap)
        def _(j):
            for mask, requester, first in groups:
                ok, c, _ = unpack(tab[requester][mask * cap + j])
                at = jnp.where(ok, requester * clusters + c, 2 * clusters)
                visit(n, chunks[n], first + j, at, ok)


def stats_kernel(plans, clusters, cap, scale, tab_a, tab_b, *refs):
    tab = (tab_a, tab_b)
    parts = len(plans)
    chunks, stats, top, total = refs[:parts], refs[parts], refs[parts + 1], refs[parts + 2]
    top[...] = jnp.full_like(top, LOW)
    total[...] = jnp.zeros_like(total)

    def raise_top(n, ref, slot, at, ok):
        top[at] = jnp.maximum(top[at], ref[slot] * scale)

    each_slot(raise_top, chunks, plans, clusters, cap, tab)
    for c in range(2 * clusters + 1):
        top[c] = jnp.broadcast_to(jnp.max(top[c], axis=-1, keepdims=True), top.shape[1:])

    def add_total(n, ref, slot, at, ok):
        total[at] = total[at] + jnp.exp(ref[slot] * scale - top[at])

    each_slot(add_total, chunks, plans, clusters, cap, tab)
    lane = lax.broadcasted_iota(jnp.int32, stats.shape, 1)
    out = jnp.zeros(stats.shape, jnp.float32)
    for c in range(2 * clusters):
        out = jnp.where(lane == c, top[c], out)
        sums = jnp.sum(total[c], axis=-1, keepdims=True)
        out = jnp.where(lane == 2 * clusters + c, sums, out)
    stats[...] = out


def weights_kernel(plans, clusters, cap, scale, tab_a, tab_b, rank, here, there, *refs):
    tab = (tab_a, tab_b)
    parts = len(plans)
    chunks, outs = refs[:parts], refs[parts : 2 * parts]
    loss, level = refs[2 * parts :]
    shape = here.shape
    row = lax.broadcasted_iota(jnp.int32, shape, 0) + rank[0] * shape[0]
    lane = lax.broadcasted_iota(jnp.int32, shape, 1)
    target = (row == lane).astype(jnp.float32)
    k = 2 * clusters
    for c in range(k):
        p = (c + clusters) % k
        top_a, top_b = here[:, c : c + 1], there[:, p : p + 1]
        sum_a, sum_b = here[:, k + c : k + c + 1], there[:, k + p : k + p + 1]
        top = jnp.maximum(top_a, top_b)
        total = sum_a * jnp.exp(top_a - top) + sum_b * jnp.exp(top_b - top)
        level[c] = jnp.broadcast_to(top + jnp.log(total), shape)
    level[k] = jnp.zeros(shape, jnp.float32)
    loss[...] = jnp.zeros(shape, jnp.float32)

    def weigh(n, ref, slot, at, ok):
        logits = ref[slot] * scale
        chances = jnp.exp(logits - level[at])
        if ok is None:
            chances = chances - target
            loss[...] += jnp.where(lane == 0, level[at], 0.0) - logits * target
        else:
            chances = jnp.where(ok, chances, 0.0)
        outs[n][slot] = chances.astype(jnp.bfloat16)

    each_slot(weigh, chunks, plans, clusters, cap, tab)


def whole_weights(pieces, order, slot):
    by_distance = sorted(zip(order, pieces), key=lambda pair: pair[0])
    return jnp.concatenate([piece[slot] for _, piece in by_distance], axis=0)


def take_pieces(refs, count, ways):
    return [refs[i * ways : (i + 1) * ways] for i in range(count)], refs[count * ways :]


def grad_kernel(tasks, used, splits, clusters, cap, order, tab_a, tab_b, rank, *refs):
    tab, ways, me = (tab_a, tab_b), len(order), rank[0]
    share = CLUSTER // ways
    mine, other = refs[:2]
    keys, at_ref = {}, 2
    for m, split in splits:
        keys[m] = refs[at_ref : at_ref + split]
        at_ref += split
    pieces, refs = take_pieces(refs[at_ref:], used, ways)
    total = refs[-1]
    come_at, out_at = 0, sum(task[3] for task in tasks)
    for kind, groups, lo, arrived, outputs in tasks:
        came = refs[come_at : come_at + arrived]
        outs = refs[out_at : out_at + outputs]
        come_at, out_at = come_at + arrived, out_at + outputs
        wide = outs[0].shape[-1]
        span = wide * outputs

        def term(n, requester, slot, mask, c, e, fresh):
            w = whole_weights(pieces[n], order, slot)
            row = rows_of(other if requester else mine, c, me, ways, slice(lo, lo + span))
            part = lax.dot_general(w, row, TN, preferred_element_type=jnp.float32)
            total[e, :, :span] = part if fresh else total[e, :, :span] + part

        def query(n, requester, slot, mask, c, e, fresh):
            w = whole_weights(pieces[n], order, slot)
            piece = keys[mask][0].shape[-1]
            for i, key in enumerate(keys[mask]):
                at = slice(i * piece, (i + 1) * piece)
                part = lax.dot_general(w, key[e], NN, preferred_element_type=jnp.float32)
                total[c, :, at] = part if fresh else total[c, :, at] + part

        visit = term if kind == "term" else query
        own = [g for g in groups if g[1:3] == (0, 0) and g[3]]
        if own:

            @pl.loop(0, clusters)
            def _(c):
                visit(own[0][0], 0, c, 0, c, c, True)

        else:
            total[:, :, :span] = jnp.zeros(total.shape[:2] + (span,), jnp.float32)

        @pl.loop(0, cap)
        def _(j):
            for n, mask, requester, first in groups:
                _, c, e = unpack(tab[requester][mask * cap + j])
                visit(n, requester, first + j, mask, c, e, False)

        @pl.loop(0, clusters)
        def _(c):
            for i, out in enumerate(outs):
                value = total[c, :, i * wide : (i + 1) * wide]
                for ref in came:
                    value = value + ref[c].astype(jnp.float32)
                if kind == "term":
                    out[c] = value.astype(out.dtype)
                else:
                    for at in range(ways):
                        block = value[at * share : (at + 1) * share]
                        out[c, share_rows(me, at, share), :] = block.astype(out.dtype)


def sum_kernel(before, base, *refs):
    parts, (out, squares) = refs[:-2], refs[-2:]
    squares[...] = before[...]

    @pl.loop(0, out.shape[0])
    def _(c):
        value = base[c]
        for ref in parts:
            if ref.shape == base.shape:
                value = value + ref[c].astype(jnp.float32)
        sides = [ref for ref in parts if ref.shape != base.shape]
        wide = out.shape[-1] // 2
        for i in range(0, len(sides), 2):
            pair = [ref[c].astype(jnp.float32) for ref in sides[i : i + 2]]
            value = value + jnp.concatenate(pair, axis=-1)
        out[c] = value
        square = jnp.sum((value * value).reshape(-1, 8, value.shape[-1]), axis=0)
        lanes = [square[:, i : i + CLUSTER] for i in range(0, value.shape[-1], CLUSTER)]
        squares[...] += sum(lanes)


def summed(before, base, *parts):
    shapes = tuple(jax.ShapeDtypeStruct(a.shape, a.dtype) for a in (base, before))
    return call("summed", sum_kernel, shapes, [], 0, (before, base, *parts), 0)


def split_of(mask):
    return 2 if mask > 1 else 1


def shards(queries, passages, matching):
    bf16, f32 = jnp.bfloat16, jnp.float32
    size, ways = lax.axis_size("dp"), lax.axis_size("tensor")
    clusters, width = matching.shape[0], queries.shape[1]
    requests = clusters * PARTNERS
    cap = -(-requests // size)
    parts = size // 2
    share = CLUSTER // ways
    scale = (width * ways) ** (-0.5)
    cube = (clusters, CLUSTER, width)
    mine, own_keys = queries.reshape(cube), passages.reshape(cube)
    here = lax.axis_index("dp").astype(jnp.int32)
    rank = lax.axis_index("tensor").astype(jnp.int32).reshape(1)
    plans = layout(parts, clusters, cap)

    halves = jnp.split(own_keys, 2, axis=-1)
    held = {}
    for bit in reversed(range(1, bits_of(parts))):
        first = swap(halves[0], "dp", 1 << bit)
        first, second = lax.optimization_barrier((first, halves[1]))
        held[1 << bit] = [first, swap(second, "dp", 1 << bit)]
        for mask in [m for m in held if m >> (bit + 1)]:
            held[mask | (1 << bit)] = [swap(h, "dp", 1 << bit) for h in held[mask]]
    if parts > 1:
        far = list(held)
        held[1] = [swap(own_keys, "dp", 1)]
    held[0] = [own_keys]
    other = swap(mine, "dp", parts)

    def table(asked):
        asked = asked.reshape(requests)
        owner, local = asked // clusters, asked % clusters
        earlier = jnp.arange(requests)[None, :] < jnp.arange(requests)[:, None]
        same = owner[:, None] == owner[None, :]
        place = (owner ^ here) * cap + jnp.sum(jnp.where(same & earlier, 1, 0), axis=1)
        code = VALID + jnp.arange(requests) // PARTNERS * 256 + local
        slots = jnp.arange(parts * cap)[:, None] == place[None, :]
        return jnp.sum(jnp.where(slots, code[None, :], 0), axis=1).astype(jnp.int32)

    tab = (table(matching), table(swap(matching, "dp", parts)))

    unit = 2 * CLUSTER * CLUSTER * width
    rows = {0: mine, 1: other}
    chunks, waits = [], ()
    for n, (groups, count) in enumerate(plans):
        if n == 1 and parts > 1:
            for mask in far:
                last, _ = lax.optimization_barrier((held[mask][-1], waits[0]))
                held[mask | 1] = [swap(h, "dp", 1) for h in held[mask][:-1] + [last]]
        masks = sorted({m for m, _, _ in groups})
        askers = sorted({r for _, r, _ in groups})
        splits = tuple((m, len(held[m])) for m in masks)
        half = jax.ShapeDtypeStruct((ways // 2, count, share, CLUSTER), f32)
        keep, give, done = call(
            f"logits_{n}",
            functools.partial(logits_kernel, groups, splits, clusters, cap, ways),
            (half, half, jax.ShapeDtypeStruct((8, CLUSTER), f32)),
            [], count * unit,
            (tab[0], tab[max(askers)], rank, *[rows[r] for r in askers],
             *[k for m in masks for k in held[m]]),
            3, waits,
        )
        waits = (done,)
        got = swap(give, "tensor", 1)
        bit = 1
        while (1 << bit) < ways:
            keep = keep + got
            pairs = keep.reshape((keep.shape[0] // 2, 2) + keep.shape[1:])
            keep = pairs[:, 0]
            got = swap(pairs[:, 1], "tensor", 1 << bit)
            bit += 1
        chunks.append((keep + got)[0])

    tile = jax.ShapeDtypeStruct((share, CLUSTER), f32)
    levels = pltpu.VMEM((2 * clusters + 1, share, CLUSTER), f32)
    stats = call(
        "row_stats",
        functools.partial(stats_kernel, plans, clusters, cap, scale),
        tile, [levels, levels], 0, (*tab, *chunks), 2,
    )
    facing = swap(stats, "dp", parts)
    *weights, loss_rows = call(
        "weights",
        functools.partial(weights_kernel, plans, clusters, cap, scale),
        [jax.ShapeDtypeStruct(chunks[n].shape, bf16) for n in range(len(plans))] + [tile],
        [levels], 0, (*tab, rank, stats, facing, *chunks), 3,
    )
    order = [0]
    for bit in reversed(range(bits_of(ways))):
        order += [at | (1 << bit) for at in order]
    pieces = [None] * len(plans)
    for n in reversed(range(len(plans))):
        pieces[n] = [weights[n]]
        for bit in reversed(range(bits_of(ways))):
            pieces[n] += [swap(piece, "tensor", 1 << bit) for piece in pieces[n]]

    def chosen(wanted):
        groups = [
            (n, m, r, first)
            for n, (plan, _) in enumerate(plans)
            for m, r, first in plan
            if wanted(m, r)
        ]
        used = sorted({g[0] for g in groups})
        groups = tuple((used.index(n), m, r, first) for n, m, r, first in groups)
        return groups, len(used), [p for n in used for p in pieces[n]]

    def gradients(name, wanted, waits=()):
        found, used, args = chosen(
            lambda m, r: any(w[1] == (m if w[0] == "term" else r) for w in wanted)
        )
        asked = sorted({g[1] for g in found}) if any(w[0] == "query" for w in wanted) else []
        tasks, shapes, came = [], [], []
        for w in wanted:
            groups = tuple(g for g in found if w[1] == (g[1] if w[0] == "term" else g[2]))
            lo, wide, outputs, add = w[2:] if w[0] == "term" else (0, width, 1, [])
            kept = bf16 if w[1] else f32
            tasks.append((w[0], groups, lo, len(add), outputs))
            shapes += [jax.ShapeDtypeStruct(cube[:2] + (wide,), kept)] * outputs
            came += add
        splits = tuple((m, len(held[m])) for m in asked)
        return call(
            name,
            functools.partial(grad_kernel, tasks, used, splits, clusters, cap, order),
            shapes, [pltpu.VMEM(cube, f32)], unit * cap * len(tasks),
            (*tab, rank, mine, other, *[k for m in asked for k in held[m]], *args, *came),
            3, waits,
        )

    def lowest(m):
        return bits_of(m & -m) if m else bits_of(parts)

    half = width // 2
    odd = [m for m in range(3, parts, 2)]
    lead = [("term", m, 0, half, 2, []) for m in odd] + [("query", 1)]
    lead += [("term", 1, 0, width, 1, [])] if parts > 1 else []
    made = gradients("grads_lead", lead)
    terms = {m: made[2 * i : 2 * i + 2] for i, m in enumerate(odd)}
    far_q, near = made[2 * len(odd)], made[2 * len(odd) + 1 :]
    own_p, own_q = gradients("grads_own", [("term", 0, 0, width, 1, []), ("query", 0)], (far_q,))
    came = []
    for m in sorted(range(2, parts, 2), key=lambda m: (lowest(m), -m)):
        came = [[swap(t, "dp", 1 << b) for t in terms[m | (1 << b)]] for b in range(lowest(m))]
        terms[m] = []
        for i in range(2):
            add = [got[i] for got in came]
            terms[m] += gradients(f"term_{m}_{i}", [("term", m, i * half, half, 1, add)])
    if near:
        if came:
            near = [lax.optimization_barrier((near[0], came[0][-1]))[0]]
        terms[1] = near
    came = [swap(t, "dp", 1 << b) for b in range(bits_of(parts)) for t in terms[1 << b]]
    far_q = swap(far_q, "dp", parts)
    zero = jnp.zeros((8, CLUSTER), f32)
    grad_q, squares = summed(zero, own_q, far_q)
    grad_p, squares = summed(squares, own_p, *came)

    sums = jnp.stack([jnp.sum(loss_rows.reshape(-1, 8, CLUSTER), axis=0), squares])
    for bit in range(bits_of(ways)):
        sums = sums + swap(sums, "tensor", 1 << bit)
    for bit in range(bits_of(size)):
        sums = sums + swap(sums, "dp", 1 << bit)
    sums = jnp.sum(sums, axis=(1, 2))
    all_rows = clusters * CLUSTER * size
    clip_limit = 0.25 * jnp.sqrt(jnp.float32(2 * all_rows * width * ways))
    factor = jnp.minimum(jnp.float32(1.0), clip_limit / jnp.sqrt(sums[1] + 1e-06))
    flat = queries.shape
    grad_queries = (grad_q * factor).astype(bf16).reshape(flat)
    grad_passages = (grad_p * factor).astype(bf16).reshape(flat)
    return (grad_queries, grad_passages, sums[0] / all_rows)


def solution(mesh):
    in_specs = (P("dp", "tensor"), P("dp", "tensor"), P("dp", None))
    out_specs = (P("dp", "tensor"), P("dp", "tensor"), P())
    return jax.shard_map(shards, mesh=mesh, in_specs=in_specs, out_specs=out_specs, check_vma=False)
```

```python
import functools

import jax
import jax.numpy as jnp
from jax import lax
from jax.experimental import pallas as pl
from jax.experimental.pallas import tpu as pltpu
from jax.sharding import PartitionSpec as P

CLUSTER = 128
PARTNERS = 8
LOW = -3.0e38
VALID = 1 << 16
VMEM_LIMIT = 56 * 1024 * 1024
SLACK = 4 * 1024 * 1024
COST = 1000
IN_CUT = 6
OUT_CUT = 4

VM = pl.BlockSpec(memory_space=pltpu.VMEM)
SM = pl.BlockSpec(memory_space=pltpu.SMEM)
ANY = pl.BlockSpec(memory_space=pl.ANY)
NT = (((1,), (1,)), ((), ()))
TN = (((0,), (0,)), ((), ()))
NN = (((1,), (0,)), ((), ()))


def bits_of(size):
    return size.bit_length() - 1


def swap(value, axis, mask):
    size = lax.axis_size(axis)
    return lax.ppermute(value, axis, [(i, i ^ mask) for i in range(size)])


def size_of(shape):
    return shape.size * shape.dtype.itemsize


def call(name, kernel, out_shape, scratch, flops, args, smem, waits=()):
    outs = jax.tree.leaves(out_shape)
    moved = sum(size_of(a) for a in args[smem:]) + sum(size_of(o) for o in outs)
    held = moved + sum(size_of(jax.ShapeDtypeStruct(x.shape, x.dtype)) for x in scratch)

    def body(*refs):
        kernel(*refs[: len(args)], *refs[len(args) + len(waits) :])

    return pl.pallas_call(
        body,
        name=name,
        out_shape=out_shape,
        in_specs=[SM] * smem + [VM] * (len(args) - smem) + [ANY] * len(waits),
        out_specs=jax.tree.map(lambda _: VM, out_shape),
        scratch_shapes=scratch,
        compiler_params=pltpu.CompilerParams(vmem_limit_bytes=min(held + SLACK, VMEM_LIMIT)),
        cost_estimate=pl.CostEstimate(flops=flops // COST, bytes_accessed=moved // COST, transcendentals=0),
    )(*args, *waits)


def unpack(code):
    return code >= VALID, (code >> 8) & 255, code & 255


def layout(parts, clusters, cap):
    plans = [
        [(m, 0) for m in range(min(parts, 2))],
        [(m, 1) for m in range(min(parts, 2))] + [(2, r) for r in (0, 1) if parts > 2],
        [(m, r) for m in range(3, parts) for r in (0, 1)],
    ]
    chunks = []
    for plan in plans:
        groups, first = [], clusters if (0, 0) in plan else 0
        for mask, requester in plan:
            groups.append((mask, requester, first))
            first += cap
        if groups:
            chunks.append((tuple(groups), first))
    return tuple(chunks)


def columns(refs):
    start = 0
    for ref in refs:
        yield ref, slice(start, start + ref.shape[-1])
        start += ref.shape[-1]


def share_rows(me, at, share):
    return pl.ds(pl.multiple_of((me ^ at) * share, share), share)


def rows_of(ref, c, me, ways, cut=slice(None)):
    share = CLUSTER // ways
    blocks = [ref[c, share_rows(me, at, share), cut] for at in range(ways)]
    return jnp.concatenate(blocks, axis=0)


def logits_kernel(groups, splits, clusters, cap, ways, tab_a, tab_b, rank, *refs):
    tab = (tab_a, tab_b)
    share = CLUSTER // ways
    me = rank[0]
    askers = sorted({r for _, r, _ in groups})
    rows = dict(zip(askers, refs))
    at_ref, keys = len(askers), {}
    for m, split in splits:
        keys[m] = refs[at_ref : at_ref + split]
        at_ref += split
    low, high, done = refs[at_ref:]
    done[...] = jnp.zeros_like(done)

    def one(row_ref, c, mask, e, slot):
        row = rows_of(row_ref, c, me, ways)
        block = None
        for key, at in columns(keys[mask]):
            part = lax.dot_general(row[:, at], key[e], NT, preferred_element_type=jnp.float32)
            block = part if block is None else block + part
        for at in range(ways):
            (high if at % 2 else low)[at // 2, slot] = block[at * share : (at + 1) * share]

    if any(first and (mask, r) == (0, 0) for mask, r, first in groups):

        @pl.loop(0, clusters)
        def _(c):
            one(rows[0], c, 0, c, c)

    @pl.loop(0, cap)
    def _(j):
        for mask, requester, first in groups:
            _, c, e = unpack(tab[requester][mask * cap + j])
            one(rows[requester], c, mask, e, first + j)


def each_slot(visit, chunks, plans, clusters, cap, tab):
    for n, (groups, _) in enumerate(plans):
        if any(first and (mask, r) == (0, 0) for mask, r, first in groups):
            for c in range(clusters):
                visit(n, chunks[n], c, c, None)

        @pl.loop(0, cap)
        def _(j):
            for mask, requester, first in groups:
                ok, c, _ = unpack(tab[requester][mask * cap + j])
                at = jnp.where(ok, requester * clusters + c, 2 * clusters)
                visit(n, chunks[n], first + j, at, ok)


def stats_kernel(plans, clusters, cap, scale, tab_a, tab_b, *refs):
    tab = (tab_a, tab_b)
    parts = len(plans)
    chunks, stats, top, total = refs[:parts], refs[parts], refs[parts + 1], refs[parts + 2]
    top[...] = jnp.full_like(top, LOW)
    total[...] = jnp.zeros_like(total)

    def raise_top(n, ref, slot, at, ok):
        top[at] = jnp.maximum(top[at], ref[slot] * scale)

    each_slot(raise_top, chunks, plans, clusters, cap, tab)
    for c in range(2 * clusters + 1):
        top[c] = jnp.broadcast_to(jnp.max(top[c], axis=-1, keepdims=True), top.shape[1:])

    def add_total(n, ref, slot, at, ok):
        total[at] = total[at] + jnp.exp(ref[slot] * scale - top[at])

    each_slot(add_total, chunks, plans, clusters, cap, tab)
    lane = lax.broadcasted_iota(jnp.int32, stats.shape, 1)
    out = jnp.zeros(stats.shape, jnp.float32)
    for c in range(2 * clusters):
        out = jnp.where(lane == c, top[c], out)
        sums = jnp.sum(total[c], axis=-1, keepdims=True)
        out = jnp.where(lane == 2 * clusters + c, sums, out)
    stats[...] = out


def weights_kernel(plans, clusters, cap, scale, tab_a, tab_b, rank, here, there, *refs):
    tab = (tab_a, tab_b)
    parts = len(plans)
    chunks, outs = refs[:parts], refs[parts : 2 * parts]
    loss, level = refs[2 * parts :]
    shape = here.shape
    row = lax.broadcasted_iota(jnp.int32, shape, 0) + rank[0] * shape[0]
    lane = lax.broadcasted_iota(jnp.int32, shape, 1)
    target = (row == lane).astype(jnp.float32)
    k = 2 * clusters
    for c in range(k):
        p = (c + clusters) % k
        top_a, top_b = here[:, c : c + 1], there[:, p : p + 1]
        sum_a, sum_b = here[:, k + c : k + c + 1], there[:, k + p : k + p + 1]
        top = jnp.maximum(top_a, top_b)
        total = sum_a * jnp.exp(top_a - top) + sum_b * jnp.exp(top_b - top)
        level[c] = jnp.broadcast_to(top + jnp.log(total), shape)
    level[k] = jnp.zeros(shape, jnp.float32)
    loss[...] = jnp.zeros(shape, jnp.float32)

    def weigh(n, ref, slot, at, ok):
        logits = ref[slot] * scale
        chances = jnp.exp(logits - level[at])
        if ok is None:
            chances = chances - target
            loss[...] += jnp.where(lane == 0, level[at], 0.0) - logits * target
        else:
            chances = jnp.where(ok, chances, 0.0)
        outs[n][slot] = chances.astype(jnp.bfloat16)

    each_slot(weigh, chunks, plans, clusters, cap, tab)


def whole_weights(pieces, order, slot):
    by_distance = sorted(zip(order, pieces), key=lambda pair: pair[0])
    return jnp.concatenate([piece[slot] for _, piece in by_distance], axis=0)


def take_pieces(refs, count, ways):
    return [refs[i * ways : (i + 1) * ways] for i in range(count)], refs[count * ways :]


def grad_kernel(tasks, used, splits, clusters, cap, order, tab_a, tab_b, rank, *refs):
    tab, ways, me = (tab_a, tab_b), len(order), rank[0]
    share = CLUSTER // ways
    mine, other = refs[:2]
    keys, at_ref = {}, 2
    for m, split in splits:
        keys[m] = refs[at_ref : at_ref + split]
        at_ref += split
    pieces, refs = take_pieces(refs[at_ref:], used, ways)
    total = refs[-1]
    come_at, out_at = 0, sum(task[3] for task in tasks)
    for kind, groups, lo, arrived, outputs in tasks:
        came = refs[come_at : come_at + arrived]
        outs = refs[out_at : out_at + outputs]
        come_at, out_at = come_at + arrived, out_at + outputs
        span = sum(out.shape[-1] for out in outs)

        def term(n, requester, slot, mask, c, e, fresh):
            w = whole_weights(pieces[n], order, slot)
            row = rows_of(other if requester else mine, c, me, ways, slice(lo, lo + span))
            part = lax.dot_general(w, row, TN, preferred_element_type=jnp.float32)
            total[e, :, :span] = part if fresh else total[e, :, :span] + part

        def query(n, requester, slot, mask, c, e, fresh):
            w = whole_weights(pieces[n], order, slot)
            for key, at in columns(keys[mask]):
                part = lax.dot_general(w, key[e], NN, preferred_element_type=jnp.float32)
                total[c, :, at] = part if fresh else total[c, :, at] + part

        visit = term if kind == "term" else query
        own = [g for g in groups if g[1:3] == (0, 0) and g[3]]
        if own:

            @pl.loop(0, clusters)
            def _(c):
                visit(own[0][0], 0, c, 0, c, c, True)

        else:
            total[:, :, :span] = jnp.zeros(total.shape[:2] + (span,), jnp.float32)

        @pl.loop(0, cap)
        def _(j):
            for n, mask, requester, first in groups:
                _, c, e = unpack(tab[requester][mask * cap + j])
                visit(n, requester, first + j, mask, c, e, False)

        @pl.loop(0, clusters)
        def _(c):
            for out, at in columns(outs):
                value = total[c, :, at]
                for ref in came:
                    value = value + ref[c].astype(jnp.float32)
                if kind == "term":
                    out[c] = value.astype(out.dtype)
                else:
                    for at in range(ways):
                        block = value[at * share : (at + 1) * share]
                        out[c, share_rows(me, at, share), :] = block.astype(out.dtype)


def sum_kernel(before, base, *refs):
    parts, (out, squares) = refs[:-2], refs[-2:]
    squares[...] = before[...]

    @pl.loop(0, out.shape[0])
    def _(c):
        value = base[c]
        for ref in parts:
            if ref.shape == base.shape:
                value = value + ref[c].astype(jnp.float32)
        sides = [ref for ref in parts if ref.shape != base.shape]
        for i in range(0, len(sides), 2):
            pair = [ref[c].astype(jnp.float32) for ref in sides[i : i + 2]]
            value = value + jnp.concatenate(pair, axis=-1)
        out[c] = value
        square = jnp.sum((value * value).reshape(-1, 8, value.shape[-1]), axis=0)
        lanes = [square[:, i : i + CLUSTER] for i in range(0, value.shape[-1], CLUSTER)]
        squares[...] += sum(lanes)


def summed(before, base, *parts):
    shapes = tuple(jax.ShapeDtypeStruct(a.shape, a.dtype) for a in (base, before))
    return call("summed", sum_kernel, shapes, [], 0, (before, base, *parts), 0)


def split_of(mask):
    return 2 if mask > 1 else 1


def shards(queries, passages, matching):
    bf16, f32 = jnp.bfloat16, jnp.float32
    size, ways = lax.axis_size("dp"), lax.axis_size("tensor")
    clusters, width = matching.shape[0], queries.shape[1]
    requests = clusters * PARTNERS
    cap = -(-requests // size)
    parts = size // 2
    share = CLUSTER // ways
    scale = (width * ways) ** (-0.5)
    cube = (clusters, CLUSTER, width)
    mine, own_keys = queries.reshape(cube), passages.reshape(cube)
    here = lax.axis_index("dp").astype(jnp.int32)
    rank = lax.axis_index("tensor").astype(jnp.int32).reshape(1)
    plans = layout(parts, clusters, cap)

    cut = max(1, width * IN_CUT // 8 // CLUSTER) * CLUSTER
    halves = jnp.split(own_keys, [cut], axis=-1)
    held = {}
    for bit in reversed(range(1, bits_of(parts))):
        first = swap(halves[0], "dp", 1 << bit)
        first, second = lax.optimization_barrier((first, halves[1]))
        held[1 << bit] = [first, swap(second, "dp", 1 << bit)]
        for mask in [m for m in held if m >> (bit + 1)]:
            held[mask | (1 << bit)] = [swap(h, "dp", 1 << bit) for h in held[mask]]
    if parts > 1:
        far = list(held)
        held[1] = [swap(own_keys, "dp", 1)]
    held[0] = [own_keys]
    other = swap(mine, "dp", parts)

    def table(asked):
        asked = asked.reshape(requests)
        owner, local = asked // clusters, asked % clusters
        earlier = jnp.arange(requests)[None, :] < jnp.arange(requests)[:, None]
        same = owner[:, None] == owner[None, :]
        place = (owner ^ here) * cap + jnp.sum(jnp.where(same & earlier, 1, 0), axis=1)
        code = VALID + jnp.arange(requests) // PARTNERS * 256 + local
        slots = jnp.arange(parts * cap)[:, None] == place[None, :]
        return jnp.sum(jnp.where(slots, code[None, :], 0), axis=1).astype(jnp.int32)

    tab = (table(matching), table(swap(matching, "dp", parts)))

    unit = 2 * CLUSTER * CLUSTER * width
    rows = {0: mine, 1: other}
    chunks, waits = [], ()
    for n, (groups, count) in enumerate(plans):
        if n == 1 and parts > 1:
            for mask in far:
                last, _ = lax.optimization_barrier((held[mask][-1], waits[0]))
                held[mask | 1] = [swap(h, "dp", 1) for h in held[mask][:-1] + [last]]
        masks = sorted({m for m, _, _ in groups})
        askers = sorted({r for _, r, _ in groups})
        splits = tuple((m, len(held[m])) for m in masks)
        half = jax.ShapeDtypeStruct((ways // 2, count, share, CLUSTER), f32)
        keep, give, done = call(
            f"logits_{n}",
            functools.partial(logits_kernel, groups, splits, clusters, cap, ways),
            (half, half, jax.ShapeDtypeStruct((8, CLUSTER), f32)),
            [], count * unit,
            (tab[0], tab[max(askers)], rank, *[rows[r] for r in askers],
             *[k for m in masks for k in held[m]]),
            3, waits,
        )
        waits = (done,)
        got = swap(give, "tensor", 1)
        bit = 1
        while (1 << bit) < ways:
            keep = keep + got
            pairs = keep.reshape((keep.shape[0] // 2, 2) + keep.shape[1:])
            keep = pairs[:, 0]
            got = swap(pairs[:, 1], "tensor", 1 << bit)
            bit += 1
        chunks.append((keep + got)[0])

    tile = jax.ShapeDtypeStruct((share, CLUSTER), f32)
    levels = pltpu.VMEM((2 * clusters + 1, share, CLUSTER), f32)
    stats = call(
        "row_stats",
        functools.partial(stats_kernel, plans, clusters, cap, scale),
        tile, [levels, levels], 0, (*tab, *chunks), 2,
    )
    facing = swap(stats, "dp", parts)
    *weights, loss_rows = call(
        "weights",
        functools.partial(weights_kernel, plans, clusters, cap, scale),
        [jax.ShapeDtypeStruct(chunks[n].shape, bf16) for n in range(len(plans))] + [tile],
        [levels], 0, (*tab, rank, stats, facing, *chunks), 3,
    )
    order = [0]
    for bit in reversed(range(bits_of(ways))):
        order += [at | (1 << bit) for at in order]
    pieces = [None] * len(plans)
    for n in reversed(range(len(plans))):
        pieces[n] = [weights[n]]
        for bit in reversed(range(bits_of(ways))):
            pieces[n] += [swap(piece, "tensor", 1 << bit) for piece in pieces[n]]

    def chosen(wanted):
        groups = [
            (n, m, r, first)
            for n, (plan, _) in enumerate(plans)
            for m, r, first in plan
            if wanted(m, r)
        ]
        used = sorted({g[0] for g in groups})
        groups = tuple((used.index(n), m, r, first) for n, m, r, first in groups)
        return groups, len(used), [p for n in used for p in pieces[n]]

    def gradients(name, wanted, waits=()):
        found, used, args = chosen(
            lambda m, r: any(w[1] == (m if w[0] == "term" else r) for w in wanted)
        )
        asked = sorted({g[1] for g in found}) if any(w[0] == "query" for w in wanted) else []
        tasks, shapes, came = [], [], []
        for w in wanted:
            groups = tuple(g for g in found if w[1] == (g[1] if w[0] == "term" else g[2]))
            lo, wides, add = w[2:] if w[0] == "term" else (0, (width,), [])
            kept = bf16 if w[1] else f32
            tasks.append((w[0], groups, lo, len(add), len(wides)))
            shapes += [jax.ShapeDtypeStruct(cube[:2] + (wide,), kept) for wide in wides]
            came += add
        splits = tuple((m, len(held[m])) for m in asked)
        return call(
            name,
            functools.partial(grad_kernel, tasks, used, splits, clusters, cap, order),
            shapes, [pltpu.VMEM(cube, f32)], unit * cap * len(tasks),
            (*tab, rank, mine, other, *[k for m in asked for k in held[m]], *args, *came),
            3, waits,
        )

    def lowest(m):
        return bits_of(m & -m) if m else bits_of(parts)

    cut = max(1, width * OUT_CUT // 8 // CLUSTER) * CLUSTER
    halves = ((0, cut), (cut, width - cut))
    odd = range(3, parts, 2)
    terms, waits = {}, ()
    if odd:
        made = gradients("terms_far", [("term", m, 0, (cut, width - cut), []) for m in odd])
        terms = {m: made[2 * i : 2 * i + 2] for i, m in enumerate(odd)}
        waits = (made[0],)
    lead = [("query", 1)] + ([("term", 1, 0, (width,), [])] if parts > 1 else [])
    far_q, *near = gradients("grads_lead", lead, waits)
    own_p, own_q = gradients("grads_own", [("term", 0, 0, (width,), []), ("query", 0)], (far_q,))
    came = []
    for m in sorted(range(2, parts, 2), key=lambda m: (lowest(m), -m)):
        came = [[swap(t, "dp", 1 << b) for t in terms[m | (1 << b)]] for b in range(lowest(m))]
        terms[m] = []
        for i, (lo, wide) in enumerate(halves):
            add = [got[i] for got in came]
            terms[m] += gradients(f"term_{m}_{i}", [("term", m, lo, (wide,), add)])
    if near:
        if came:
            near = [lax.optimization_barrier((near[0], came[0][-1]))[0]]
        terms[1] = near
    came = [swap(t, "dp", 1 << b) for b in range(bits_of(parts)) for t in terms[1 << b]]
    far_q = swap(far_q, "dp", parts)
    zero = jnp.zeros((8, CLUSTER), f32)
    grad_q, squares = summed(zero, own_q, far_q)
    grad_p, squares = summed(squares, own_p, *came)

    sums = jnp.stack([jnp.sum(loss_rows.reshape(-1, 8, CLUSTER), axis=0), squares])
    for bit in range(bits_of(ways)):
        sums = sums + swap(sums, "tensor", 1 << bit)
    for bit in range(bits_of(size)):
        sums = sums + swap(sums, "dp", 1 << bit)
    sums = jnp.sum(sums, axis=(1, 2))
    all_rows = clusters * CLUSTER * size
    clip_limit = 0.25 * jnp.sqrt(jnp.float32(2 * all_rows * width * ways))
    factor = jnp.minimum(jnp.float32(1.0), clip_limit / jnp.sqrt(sums[1] + 1e-06))
    flat = queries.shape
    grad_queries = (grad_q * factor).astype(bf16).reshape(flat)
    grad_passages = (grad_p * factor).astype(bf16).reshape(flat)
    return (grad_queries, grad_passages, sums[0] / all_rows)


def solution(mesh):
    in_specs = (P("dp", "tensor"), P("dp", "tensor"), P("dp", None))
    out_specs = (P("dp", "tensor"), P("dp", "tensor"), P())
    return jax.shard_map(shards, mesh=mesh, in_specs=in_specs, out_specs=out_specs, check_vma=False)
```

```python
import functools

import jax
import jax.numpy as jnp
from jax import lax
from jax.experimental import pallas as pl
from jax.experimental.pallas import tpu as pltpu
from jax.sharding import PartitionSpec as P

CLUSTER = 128
PARTNERS = 8
LOW = -3.0e38
VALID = 1 << 16
VMEM_LIMIT = 56 * 1024 * 1024
SLACK = 4 * 1024 * 1024
COST = 1000
IN_CUT = 6
OUT_CUT = 4

VM = pl.BlockSpec(memory_space=pltpu.VMEM)
SM = pl.BlockSpec(memory_space=pltpu.SMEM)
ANY = pl.BlockSpec(memory_space=pl.ANY)
NT = (((1,), (1,)), ((), ()))
TN = (((0,), (0,)), ((), ()))
NN = (((1,), (0,)), ((), ()))


def bits_of(size):
    return size.bit_length() - 1


def swap(value, axis, mask):
    size = lax.axis_size(axis)
    return lax.ppermute(value, axis, [(i, i ^ mask) for i in range(size)])


def size_of(shape):
    return shape.size * shape.dtype.itemsize


def call(name, kernel, out_shape, scratch, flops, args, smem, waits=()):
    outs = jax.tree.leaves(out_shape)
    moved = sum(size_of(a) for a in args[smem:]) + sum(size_of(o) for o in outs)
    held = moved + sum(size_of(jax.ShapeDtypeStruct(x.shape, x.dtype)) for x in scratch)

    def body(*refs):
        kernel(*refs[: len(args)], *refs[len(args) + len(waits) :])

    return pl.pallas_call(
        body,
        name=name,
        out_shape=out_shape,
        in_specs=[SM] * smem + [VM] * (len(args) - smem) + [ANY] * len(waits),
        out_specs=jax.tree.map(lambda _: VM, out_shape),
        scratch_shapes=scratch,
        compiler_params=pltpu.CompilerParams(vmem_limit_bytes=min(held + SLACK, VMEM_LIMIT)),
        cost_estimate=pl.CostEstimate(flops=flops // COST, bytes_accessed=moved // COST, transcendentals=0),
    )(*args, *waits)


def unpack(code):
    return code >= VALID, (code >> 8) & 255, code & 255


def layout(parts, clusters, cap):
    plans = [
        [(m, 0) for m in range(min(parts, 2))],
        [(m, 1) for m in range(min(parts, 2))] + [(2, r) for r in (0, 1) if parts > 2],
        [(m, r) for m in range(3, parts) for r in (0, 1)],
    ]
    chunks = []
    for plan in plans:
        groups, first = [], clusters if (0, 0) in plan else 0
        for mask, requester in plan:
            groups.append((mask, requester, first))
            first += cap
        if groups:
            chunks.append((tuple(groups), first))
    return tuple(chunks)


def columns(refs):
    start = 0
    for ref in refs:
        yield ref, slice(start, start + ref.shape[-1])
        start += ref.shape[-1]


def share_rows(me, at, share):
    return pl.ds(pl.multiple_of((me ^ at) * share, share), share)


def rows_of(ref, c, me, ways, cut=slice(None)):
    share = CLUSTER // ways
    blocks = [ref[c, share_rows(me, at, share), cut] for at in range(ways)]
    return jnp.concatenate(blocks, axis=0)


def logits_kernel(groups, splits, clusters, cap, ways, tab_a, tab_b, rank, *refs):
    tab = (tab_a, tab_b)
    share = CLUSTER // ways
    me = rank[0]
    askers = sorted({r for _, r, _ in groups})
    rows = dict(zip(askers, refs))
    at_ref, keys = len(askers), {}
    for m, split in splits:
        keys[m] = refs[at_ref : at_ref + split]
        at_ref += split
    low, high, done = refs[at_ref:]
    done[...] = jnp.zeros_like(done)

    def one(row_ref, c, mask, e, slot):
        row = rows_of(row_ref, c, me, ways)
        block = None
        for key, at in columns(keys[mask]):
            part = lax.dot_general(row[:, at], key[e], NT, preferred_element_type=jnp.float32)
            block = part if block is None else block + part
        for at in range(ways):
            (high if at % 2 else low)[at // 2, slot] = block[at * share : (at + 1) * share]

    if any(first and (mask, r) == (0, 0) for mask, r, first in groups):

        @pl.loop(0, clusters)
        def _(c):
            one(rows[0], c, 0, c, c)

    @pl.loop(0, cap)
    def _(j):
        for mask, requester, first in groups:
            _, c, e = unpack(tab[requester][mask * cap + j])
            one(rows[requester], c, mask, e, first + j)


def each_slot(visit, chunks, plans, clusters, cap, tab):
    for n, (groups, _) in enumerate(plans):
        if any(first and (mask, r) == (0, 0) for mask, r, first in groups):
            for c in range(clusters):
                visit(n, chunks[n], c, c, None)

        @pl.loop(0, cap)
        def _(j):
            for mask, requester, first in groups:
                ok, c, _ = unpack(tab[requester][mask * cap + j])
                at = jnp.where(ok, requester * clusters + c, 2 * clusters)
                visit(n, chunks[n], first + j, at, ok)


def stats_kernel(plans, clusters, cap, scale, tab_a, tab_b, *refs):
    tab = (tab_a, tab_b)
    parts = len(plans)
    chunks, stats, top, total = refs[:parts], refs[parts], refs[parts + 1], refs[parts + 2]
    top[...] = jnp.full_like(top, LOW)
    total[...] = jnp.zeros_like(total)

    def raise_top(n, ref, slot, at, ok):
        top[at] = jnp.maximum(top[at], ref[slot] * scale)

    each_slot(raise_top, chunks, plans, clusters, cap, tab)
    for c in range(2 * clusters + 1):
        top[c] = jnp.broadcast_to(jnp.max(top[c], axis=-1, keepdims=True), top.shape[1:])

    def add_total(n, ref, slot, at, ok):
        total[at] = total[at] + jnp.exp(ref[slot] * scale - top[at])

    each_slot(add_total, chunks, plans, clusters, cap, tab)
    lane = lax.broadcasted_iota(jnp.int32, stats.shape, 1)
    out = jnp.zeros(stats.shape, jnp.float32)
    for c in range(2 * clusters):
        out = jnp.where(lane == c, top[c], out)
        sums = jnp.sum(total[c], axis=-1, keepdims=True)
        out = jnp.where(lane == 2 * clusters + c, sums, out)
    stats[...] = out


def weights_kernel(plans, clusters, cap, scale, tab_a, tab_b, rank, here, there, *refs):
    tab = (tab_a, tab_b)
    parts = len(plans)
    chunks, outs = refs[:parts], refs[parts : 2 * parts]
    loss, level = refs[2 * parts :]
    shape = here.shape
    row = lax.broadcasted_iota(jnp.int32, shape, 0) + rank[0] * shape[0]
    lane = lax.broadcasted_iota(jnp.int32, shape, 1)
    target = (row == lane).astype(jnp.float32)
    k = 2 * clusters
    for c in range(k):
        p = (c + clusters) % k
        top_a, top_b = here[:, c : c + 1], there[:, p : p + 1]
        sum_a, sum_b = here[:, k + c : k + c + 1], there[:, k + p : k + p + 1]
        top = jnp.maximum(top_a, top_b)
        total = sum_a * jnp.exp(top_a - top) + sum_b * jnp.exp(top_b - top)
        level[c] = jnp.broadcast_to(top + jnp.log(total), shape)
    level[k] = jnp.zeros(shape, jnp.float32)
    loss[...] = jnp.zeros(shape, jnp.float32)

    def weigh(n, ref, slot, at, ok):
        logits = ref[slot] * scale
        chances = jnp.exp(logits - level[at])
        if ok is None:
            chances = chances - target
            loss[...] += jnp.where(lane == 0, level[at], 0.0) - logits * target
        else:
            chances = jnp.where(ok, chances, 0.0)
        outs[n][slot] = chances.astype(jnp.bfloat16)

    each_slot(weigh, chunks, plans, clusters, cap, tab)


def whole_weights(pieces, order, slot):
    by_distance = sorted(zip(order, pieces), key=lambda pair: pair[0])
    return jnp.concatenate([piece[slot] for _, piece in by_distance], axis=0)


def take_pieces(refs, count, ways):
    return [refs[i * ways : (i + 1) * ways] for i in range(count)], refs[count * ways :]


def grad_kernel(tasks, used, splits, clusters, cap, order, tab_a, tab_b, rank, *refs):
    tab, ways, me = (tab_a, tab_b), len(order), rank[0]
    share = CLUSTER // ways
    mine, other = refs[:2]
    keys, at_ref = {}, 2
    for m, split in splits:
        keys[m] = refs[at_ref : at_ref + split]
        at_ref += split
    pieces, refs = take_pieces(refs[at_ref:], used, ways)
    total = refs[-1]
    come_at, out_at = 0, sum(task[3] for task in tasks)
    for kind, groups, lo, arrived, outputs in tasks:
        came = refs[come_at : come_at + arrived]
        outs = refs[out_at : out_at + outputs]
        come_at, out_at = come_at + arrived, out_at + outputs
        span = sum(out.shape[-1] for out in outs)

        def term(n, requester, slot, mask, c, e, fresh):
            w = whole_weights(pieces[n], order, slot)
            row = rows_of(other if requester else mine, c, me, ways, slice(lo, lo + span))
            part = lax.dot_general(w, row, TN, preferred_element_type=jnp.float32)
            total[e, :, :span] = part if fresh else total[e, :, :span] + part

        def query(n, requester, slot, mask, c, e, fresh):
            w = whole_weights(pieces[n], order, slot)
            for key, at in columns(keys[mask]):
                part = lax.dot_general(w, key[e], NN, preferred_element_type=jnp.float32)
                total[c, :, at] = part if fresh else total[c, :, at] + part

        visit = term if kind == "term" else query
        own = [g for g in groups if g[1:3] == (0, 0) and g[3]]
        if own:

            @pl.loop(0, clusters)
            def _(c):
                visit(own[0][0], 0, c, 0, c, c, True)

        else:
            total[:, :, :span] = jnp.zeros(total.shape[:2] + (span,), jnp.float32)

        @pl.loop(0, cap)
        def _(j):
            for n, mask, requester, first in groups:
                _, c, e = unpack(tab[requester][mask * cap + j])
                visit(n, requester, first + j, mask, c, e, False)

        @pl.loop(0, clusters)
        def _(c):
            for out, at in columns(outs):
                value = total[c, :, at]
                for ref in came:
                    value = value + ref[c].astype(jnp.float32)
                if kind == "term":
                    out[c] = value.astype(out.dtype)
                else:
                    for at in range(ways):
                        block = value[at * share : (at + 1) * share]
                        out[c, share_rows(me, at, share), :] = block.astype(out.dtype)


def sum_kernel(before, base, *refs):
    parts, (out, squares) = refs[:-2], refs[-2:]
    squares[...] = before[...]

    @pl.loop(0, out.shape[0])
    def _(c):
        value = base[c]
        for ref in parts:
            if ref.shape == base.shape:
                value = value + ref[c].astype(jnp.float32)
        sides = [ref for ref in parts if ref.shape != base.shape]
        for i in range(0, len(sides), 2):
            pair = [ref[c].astype(jnp.float32) for ref in sides[i : i + 2]]
            value = value + jnp.concatenate(pair, axis=-1)
        out[c] = value
        square = jnp.sum((value * value).reshape(-1, 8, value.shape[-1]), axis=0)
        lanes = [square[:, i : i + CLUSTER] for i in range(0, value.shape[-1], CLUSTER)]
        squares[...] += sum(lanes)


def summed(before, base, *parts):
    shapes = tuple(jax.ShapeDtypeStruct(a.shape, a.dtype) for a in (base, before))
    return call("summed", sum_kernel, shapes, [], 0, (before, base, *parts), 0)


def split_of(mask):
    return 2 if mask > 1 else 1


def shards(queries, passages, matching):
    bf16, f32 = jnp.bfloat16, jnp.float32
    size, ways = lax.axis_size("dp"), lax.axis_size("tensor")
    clusters, width = matching.shape[0], queries.shape[1]
    requests = clusters * PARTNERS
    cap = -(-requests // size)
    parts = size // 2
    share = CLUSTER // ways
    scale = (width * ways) ** (-0.5)
    cube = (clusters, CLUSTER, width)
    mine, own_keys = queries.reshape(cube), passages.reshape(cube)
    here = lax.axis_index("dp").astype(jnp.int32)
    rank = lax.axis_index("tensor").astype(jnp.int32).reshape(1)
    plans = layout(parts, clusters, cap)

    cut = max(1, width * IN_CUT // 8 // CLUSTER) * CLUSTER
    halves = jnp.split(own_keys, [cut], axis=-1)
    held = {}
    for bit in reversed(range(1, bits_of(parts))):
        first = swap(halves[0], "dp", 1 << bit)
        first, second = lax.optimization_barrier((first, halves[1]))
        held[1 << bit] = [first, swap(second, "dp", 1 << bit)]
        for mask in [m for m in held if m >> (bit + 1)]:
            held[mask | (1 << bit)] = [swap(h, "dp", 1 << bit) for h in held[mask]]
    if parts > 1:
        far = list(held)
        held[1] = [swap(own_keys, "dp", 1)]
    held[0] = [own_keys]
    other = swap(mine, "dp", parts)
    step = jnp.zeros((8, CLUSTER), jnp.float32)
    for _ in range(1):
        step, _ = lax.optimization_barrier((step, other))
        step = swap(step, "tensor", 1)
    other, _ = lax.optimization_barrier((other, step))

    def table(asked):
        asked = asked.reshape(requests)
        owner, local = asked // clusters, asked % clusters
        earlier = jnp.arange(requests)[None, :] < jnp.arange(requests)[:, None]
        same = owner[:, None] == owner[None, :]
        place = (owner ^ here) * cap + jnp.sum(jnp.where(same & earlier, 1, 0), axis=1)
        code = VALID + jnp.arange(requests) // PARTNERS * 256 + local
        slots = jnp.arange(parts * cap)[:, None] == place[None, :]
        return jnp.sum(jnp.where(slots, code[None, :], 0), axis=1).astype(jnp.int32)

    tab = (table(matching), table(swap(matching, "dp", parts)))

    unit = 2 * CLUSTER * CLUSTER * width
    rows = {0: mine, 1: other}
    chunks, waits = [], (tab[1],)
    for n, (groups, count) in enumerate(plans):
        if n == 1 and parts > 1:
            for mask in far:
                last, _ = lax.optimization_barrier((held[mask][-1], waits[0]))
                held[mask | 1] = [swap(h, "dp", 1) for h in held[mask][:-1] + [last]]
        masks = sorted({m for m, _, _ in groups})
        askers = sorted({r for _, r, _ in groups})
        splits = tuple((m, len(held[m])) for m in masks)
        half = jax.ShapeDtypeStruct((ways // 2, count, share, CLUSTER), f32)
        keep, give, done = call(
            f"logits_{n}",
            functools.partial(logits_kernel, groups, splits, clusters, cap, ways),
            (half, half, jax.ShapeDtypeStruct((8, CLUSTER), f32)),
            [], count * unit,
            (tab[0], tab[max(askers)], rank, *[rows[r] for r in askers],
             *[k for m in masks for k in held[m]]),
            3, waits,
        )
        waits = (done,)
        got = swap(give, "tensor", 1)
        bit = 1
        while (1 << bit) < ways:
            keep = keep + got
            pairs = keep.reshape((keep.shape[0] // 2, 2) + keep.shape[1:])
            keep = pairs[:, 0]
            got = swap(pairs[:, 1], "tensor", 1 << bit)
            bit += 1
        chunks.append((keep + got)[0])
        waits += (chunks[0],) if len(chunks) == 1 else ()

    tile = jax.ShapeDtypeStruct((share, CLUSTER), f32)
    levels = pltpu.VMEM((2 * clusters + 1, share, CLUSTER), f32)
    stats = call(
        "row_stats",
        functools.partial(stats_kernel, plans, clusters, cap, scale),
        tile, [levels, levels], 0, (*tab, *chunks), 2,
    )
    facing = swap(stats, "dp", parts)
    *weights, loss_rows = call(
        "weights",
        functools.partial(weights_kernel, plans, clusters, cap, scale),
        [jax.ShapeDtypeStruct(chunks[n].shape, bf16) for n in range(len(plans))] + [tile],
        [levels], 0, (*tab, rank, stats, facing, *chunks), 3,
    )
    order = [0]
    for bit in reversed(range(bits_of(ways))):
        order += [at | (1 << bit) for at in order]
    pieces = [None] * len(plans)
    for n in reversed(range(len(plans))):
        pieces[n] = [weights[n]]
        for bit in reversed(range(bits_of(ways))):
            pieces[n] += [swap(piece, "tensor", 1 << bit) for piece in pieces[n]]

    def chosen(wanted):
        groups = [
            (n, m, r, first)
            for n, (plan, _) in enumerate(plans)
            for m, r, first in plan
            if wanted(m, r)
        ]
        used = sorted({g[0] for g in groups})
        groups = tuple((used.index(n), m, r, first) for n, m, r, first in groups)
        return groups, len(used), [p for n in used for p in pieces[n]]

    def gradients(name, wanted, waits=()):
        found, used, args = chosen(
            lambda m, r: any(w[1] == (m if w[0] == "term" else r) for w in wanted)
        )
        asked = sorted({g[1] for g in found}) if any(w[0] == "query" for w in wanted) else []
        tasks, shapes, came = [], [], []
        for w in wanted:
            groups = tuple(g for g in found if w[1] == (g[1] if w[0] == "term" else g[2]))
            lo, wides, add = w[2:] if w[0] == "term" else (0, (width,), [])
            kept = bf16 if w[1] else f32
            tasks.append((w[0], groups, lo, len(add), len(wides)))
            shapes += [jax.ShapeDtypeStruct(cube[:2] + (wide,), kept) for wide in wides]
            came += add
        splits = tuple((m, len(held[m])) for m in asked)
        return call(
            name,
            functools.partial(grad_kernel, tasks, used, splits, clusters, cap, order),
            shapes, [pltpu.VMEM(cube, f32)], unit * cap * len(tasks),
            (*tab, rank, mine, other, *[k for m in asked for k in held[m]], *args, *came),
            3, waits,
        )

    def lowest(m):
        return bits_of(m & -m) if m else bits_of(parts)

    cut = max(1, width * OUT_CUT // 8 // CLUSTER) * CLUSTER
    halves = ((0, cut), (cut, width - cut))
    odd = range(3, parts, 2)
    terms, waits = {}, ()
    if odd:
        made = gradients("terms_far", [("term", m, 0, (cut, width - cut), []) for m in odd])
        terms = {m: made[2 * i : 2 * i + 2] for i, m in enumerate(odd)}
        waits = (made[0],)
    lead = [("query", 1)] + ([("term", 1, 0, (width,), [])] if parts > 1 else [])
    far_q, *near = gradients("grads_lead", lead, waits)
    own_p, own_q = gradients("grads_own", [("term", 0, 0, (width,), []), ("query", 0)], (far_q,))
    came = []
    for m in sorted(range(2, parts, 2), key=lambda m: (lowest(m), -m)):
        came = [[swap(t, "dp", 1 << b) for t in terms[m | (1 << b)]] for b in range(lowest(m))]
        terms[m] = []
        for i, (lo, wide) in enumerate(halves):
            add = [got[i] for got in came]
            terms[m] += gradients(f"term_{m}_{i}", [("term", m, lo, (wide,), add)])
    if near:
        if came:
            near = [lax.optimization_barrier((near[0], came[0][-1]))[0]]
        terms[1] = near
    came = [swap(t, "dp", 1 << b) for b in range(bits_of(parts)) for t in terms[1 << b]]
    far_q = swap(far_q, "dp", parts)
    zero = jnp.zeros((8, CLUSTER), f32)
    grad_q, squares = summed(zero, own_q, far_q)
    grad_p, squares = summed(squares, own_p, *came)

    sums = jnp.stack([jnp.sum(loss_rows.reshape(-1, 8, CLUSTER), axis=0), squares])
    for bit in range(bits_of(ways)):
        sums = sums + swap(sums, "tensor", 1 << bit)
    for bit in range(bits_of(size)):
        sums = sums + swap(sums, "dp", 1 << bit)
    sums = jnp.sum(sums, axis=(1, 2))
    all_rows = clusters * CLUSTER * size
    clip_limit = 0.25 * jnp.sqrt(jnp.float32(2 * all_rows * width * ways))
    factor = jnp.minimum(jnp.float32(1.0), clip_limit / jnp.sqrt(sums[1] + 1e-06))
    flat = queries.shape
    grad_queries = (grad_q * factor).astype(bf16).reshape(flat)
    grad_passages = (grad_p * factor).astype(bf16).reshape(flat)
    return (grad_queries, grad_passages, sums[0] / all_rows)


def solution(mesh):
    in_specs = (P("dp", "tensor"), P("dp", "tensor"), P("dp", None))
    out_specs = (P("dp", "tensor"), P("dp", "tensor"), P())
    return jax.shard_map(shards, mesh=mesh, in_specs=in_specs, out_specs=out_specs, check_vma=False)
```

```python
import functools

import jax
import jax.numpy as jnp
from jax import lax
from jax.experimental import pallas as pl
from jax.experimental.pallas import tpu as pltpu
from jax.sharding import PartitionSpec as P

CLUSTER = 128
PARTNERS = 8
LOW = -3.0e38
VALID = 1 << 16
VMEM_LIMIT = 56 * 1024 * 1024
SLACK = 4 * 1024 * 1024
COST = 1
IN_CUT = 6
OUT_CUT = 4

VM = pl.BlockSpec(memory_space=pltpu.VMEM)
SM = pl.BlockSpec(memory_space=pltpu.SMEM)
ANY = pl.BlockSpec(memory_space=pl.ANY)
NT = (((1,), (1,)), ((), ()))
TN = (((0,), (0,)), ((), ()))
NN = (((1,), (0,)), ((), ()))


def bits_of(size):
    return size.bit_length() - 1


def swap(value, axis, mask):
    size = lax.axis_size(axis)
    return lax.ppermute(value, axis, [(i, i ^ mask) for i in range(size)])


def size_of(shape):
    return shape.size * shape.dtype.itemsize


def call(name, kernel, out_shape, scratch, flops, args, smem, waits=()):
    outs = jax.tree.leaves(out_shape)
    moved = sum(size_of(a) for a in args[smem:]) + sum(size_of(o) for o in outs)
    held = moved + sum(size_of(jax.ShapeDtypeStruct(x.shape, x.dtype)) for x in scratch)

    def body(*refs):
        kernel(*refs[: len(args)], *refs[len(args) + len(waits) :])

    return pl.pallas_call(
        body,
        name=name,
        out_shape=out_shape,
        in_specs=[SM] * smem + [VM] * (len(args) - smem) + [ANY] * len(waits),
        out_specs=jax.tree.map(lambda _: VM, out_shape),
        scratch_shapes=scratch,
        compiler_params=pltpu.CompilerParams(vmem_limit_bytes=min(held + SLACK, VMEM_LIMIT)),
        cost_estimate=pl.CostEstimate(flops=flops // COST, bytes_accessed=moved // COST, transcendentals=0),
    )(*args, *waits)


def unpack(code):
    return code >= VALID, (code >> 8) & 255, code & 255


def layout(parts, clusters, cap):
    plans = [
        [(m, 0) for m in range(min(parts, 2))],
        [(m, 1) for m in range(min(parts, 2))] + [(2, r) for r in (0, 1) if parts > 2],
        [(m, r) for m in range(3, parts) for r in (0, 1)],
    ]
    chunks = []
    for plan in plans:
        groups, first = [], clusters if (0, 0) in plan else 0
        for mask, requester in plan:
            groups.append((mask, requester, first))
            first += cap
        if groups:
            chunks.append((tuple(groups), first))
    return tuple(chunks)


def columns(refs):
    start = 0
    for ref in refs:
        yield ref, slice(start, start + ref.shape[-1])
        start += ref.shape[-1]


def share_rows(me, at, share):
    return pl.ds(pl.multiple_of((me ^ at) * share, share), share)


def rows_of(ref, c, me, ways, cut=slice(None)):
    share = CLUSTER // ways
    blocks = [ref[c, share_rows(me, at, share), cut] for at in range(ways)]
    return jnp.concatenate(blocks, axis=0)


def logits_kernel(groups, splits, clusters, cap, ways, tab_a, tab_b, rank, *refs):
    tab = (tab_a, tab_b)
    share = CLUSTER // ways
    me = rank[0]
    askers = sorted({r for _, r, _ in groups})
    rows = dict(zip(askers, refs))
    at_ref, keys = len(askers), {}
    for m, split in splits:
        keys[m] = refs[at_ref : at_ref + split]
        at_ref += split
    low, high, done = refs[at_ref:]
    done[...] = jnp.zeros_like(done)

    def one(row_ref, c, mask, e, slot):
        row = rows_of(row_ref, c, me, ways)
        block = None
        for key, at in columns(keys[mask]):
            part = lax.dot_general(row[:, at], key[e], NT, preferred_element_type=jnp.float32)
            block = part if block is None else block + part
        for at in range(ways):
            (high if at % 2 else low)[at // 2, slot] = block[at * share : (at + 1) * share]

    if any(first and (mask, r) == (0, 0) for mask, r, first in groups):

        @pl.loop(0, clusters)
        def _(c):
            one(rows[0], c, 0, c, c)

    @pl.loop(0, cap)
    def _(j):
        for mask, requester, first in groups:
            _, c, e = unpack(tab[requester][mask * cap + j])
            one(rows[requester], c, mask, e, first + j)


def each_slot(visit, chunks, plans, clusters, cap, tab):
    for n, (groups, _) in enumerate(plans):
        if any(first and (mask, r) == (0, 0) for mask, r, first in groups):
            for c in range(clusters):
                visit(n, chunks[n], c, c, None)

        @pl.loop(0, cap)
        def _(j):
            for mask, requester, first in groups:
                ok, c, _ = unpack(tab[requester][mask * cap + j])
                at = jnp.where(ok, requester * clusters + c, 2 * clusters)
                visit(n, chunks[n], first + j, at, ok)


def stats_kernel(plans, clusters, cap, scale, tab_a, tab_b, *refs):
    tab = (tab_a, tab_b)
    parts = len(plans)
    chunks, stats, top, total = refs[:parts], refs[parts], refs[parts + 1], refs[parts + 2]
    top[...] = jnp.full_like(top, LOW)
    total[...] = jnp.zeros_like(total)

    def raise_top(n, ref, slot, at, ok):
        top[at] = jnp.maximum(top[at], ref[slot] * scale)

    each_slot(raise_top, chunks, plans, clusters, cap, tab)
    for c in range(2 * clusters + 1):
        top[c] = jnp.broadcast_to(jnp.max(top[c], axis=-1, keepdims=True), top.shape[1:])

    def add_total(n, ref, slot, at, ok):
        total[at] = total[at] + jnp.exp(ref[slot] * scale - top[at])

    each_slot(add_total, chunks, plans, clusters, cap, tab)
    lane = lax.broadcasted_iota(jnp.int32, stats.shape, 1)
    out = jnp.zeros(stats.shape, jnp.float32)
    for c in range(2 * clusters):
        out = jnp.where(lane == c, top[c], out)
        sums = jnp.sum(total[c], axis=-1, keepdims=True)
        out = jnp.where(lane == 2 * clusters + c, sums, out)
    stats[...] = out


def weights_kernel(plans, clusters, cap, scale, tab_a, tab_b, rank, here, there, *refs):
    tab = (tab_a, tab_b)
    parts = len(plans)
    chunks, outs = refs[:parts], refs[parts : 2 * parts]
    loss, level = refs[2 * parts :]
    shape = here.shape
    row = lax.broadcasted_iota(jnp.int32, shape, 0) + rank[0] * shape[0]
    lane = lax.broadcasted_iota(jnp.int32, shape, 1)
    target = (row == lane).astype(jnp.float32)
    k = 2 * clusters
    for c in range(k):
        p = (c + clusters) % k
        top_a, top_b = here[:, c : c + 1], there[:, p : p + 1]
        sum_a, sum_b = here[:, k + c : k + c + 1], there[:, k + p : k + p + 1]
        top = jnp.maximum(top_a, top_b)
        total = sum_a * jnp.exp(top_a - top) + sum_b * jnp.exp(top_b - top)
        level[c] = jnp.broadcast_to(top + jnp.log(total), shape)
    level[k] = jnp.zeros(shape, jnp.float32)
    loss[...] = jnp.zeros(shape, jnp.float32)

    def weigh(n, ref, slot, at, ok):
        logits = ref[slot] * scale
        chances = jnp.exp(logits - level[at])
        if ok is None:
            chances = chances - target
            loss[...] += jnp.where(lane == 0, level[at], 0.0) - logits * target
        else:
            chances = jnp.where(ok, chances, 0.0)
        outs[n][slot] = chances.astype(jnp.bfloat16)

    each_slot(weigh, chunks, plans, clusters, cap, tab)


def whole_weights(pieces, order, slot):
    by_distance = sorted(zip(order, pieces), key=lambda pair: pair[0])
    return jnp.concatenate([piece[slot] for _, piece in by_distance], axis=0)


def take_pieces(refs, count, ways):
    return [refs[i * ways : (i + 1) * ways] for i in range(count)], refs[count * ways :]


def grad_kernel(tasks, used, splits, clusters, cap, order, tab_a, tab_b, rank, *refs):
    tab, ways, me = (tab_a, tab_b), len(order), rank[0]
    share = CLUSTER // ways
    mine, other = refs[:2]
    keys, at_ref = {}, 2
    for m, split in splits:
        keys[m] = refs[at_ref : at_ref + split]
        at_ref += split
    pieces, refs = take_pieces(refs[at_ref:], used, ways)
    total = refs[-1]
    come_at, out_at = 0, sum(task[3] for task in tasks)
    for kind, groups, lo, arrived, outputs in tasks:
        came = refs[come_at : come_at + arrived]
        outs = refs[out_at : out_at + outputs]
        come_at, out_at = come_at + arrived, out_at + outputs
        span = sum(out.shape[-1] for out in outs)

        def term(n, requester, slot, mask, c, e, fresh):
            w = whole_weights(pieces[n], order, slot)
            row = rows_of(other if requester else mine, c, me, ways, slice(lo, lo + span))
            part = lax.dot_general(w, row, TN, preferred_element_type=jnp.float32)
            total[e, :, :span] = part if fresh else total[e, :, :span] + part

        def query(n, requester, slot, mask, c, e, fresh):
            w = whole_weights(pieces[n], order, slot)
            for key, at in columns(keys[mask]):
                part = lax.dot_general(w, key[e], NN, preferred_element_type=jnp.float32)
                total[c, :, at] = part if fresh else total[c, :, at] + part

        visit = term if kind == "term" else query
        own = [g for g in groups if g[1:3] == (0, 0) and g[3]]
        if own:

            @pl.loop(0, clusters)
            def _(c):
                visit(own[0][0], 0, c, 0, c, c, True)

        else:
            total[:, :, :span] = jnp.zeros(total.shape[:2] + (span,), jnp.float32)

        @pl.loop(0, cap)
        def _(j):
            for n, mask, requester, first in groups:
                _, c, e = unpack(tab[requester][mask * cap + j])
                visit(n, requester, first + j, mask, c, e, False)

        @pl.loop(0, clusters)
        def _(c):
            for out, at in columns(outs):
                value = total[c, :, at]
                for ref in came:
                    value = value + ref[c].astype(jnp.float32)
                if kind == "term":
                    out[c] = value.astype(out.dtype)
                else:
                    for at in range(ways):
                        block = value[at * share : (at + 1) * share]
                        out[c, share_rows(me, at, share), :] = block.astype(out.dtype)


def sum_kernel(before, base, *refs):
    parts, (out, squares) = refs[:-2], refs[-2:]
    squares[...] = before[...]

    @pl.loop(0, out.shape[0])
    def _(c):
        value = base[c]
        for ref in parts:
            if ref.shape == base.shape:
                value = value + ref[c].astype(jnp.float32)
        sides = [ref for ref in parts if ref.shape != base.shape]
        for i in range(0, len(sides), 2):
            pair = [ref[c].astype(jnp.float32) for ref in sides[i : i + 2]]
            value = value + jnp.concatenate(pair, axis=-1)
        out[c] = value
        square = jnp.sum((value * value).reshape(-1, 8, value.shape[-1]), axis=0)
        lanes = [square[:, i : i + CLUSTER] for i in range(0, value.shape[-1], CLUSTER)]
        squares[...] += sum(lanes)


def summed(before, base, *parts):
    shapes = tuple(jax.ShapeDtypeStruct(a.shape, a.dtype) for a in (base, before))
    return call("summed", sum_kernel, shapes, [], 0, (before, base, *parts), 0)


def split_of(mask):
    return 2 if mask > 1 else 1


def shards(queries, passages, matching):
    bf16, f32 = jnp.bfloat16, jnp.float32
    size, ways = lax.axis_size("dp"), lax.axis_size("tensor")
    clusters, width = matching.shape[0], queries.shape[1]
    requests = clusters * PARTNERS
    cap = -(-requests // size)
    parts = size // 2
    share = CLUSTER // ways
    scale = (width * ways) ** (-0.5)
    cube = (clusters, CLUSTER, width)
    mine, own_keys = queries.reshape(cube), passages.reshape(cube)
    here = lax.axis_index("dp").astype(jnp.int32)
    rank = lax.axis_index("tensor").astype(jnp.int32).reshape(1)
    plans = layout(parts, clusters, cap)

    cut = max(1, width * IN_CUT // 8 // CLUSTER) * CLUSTER
    halves = jnp.split(own_keys, [cut], axis=-1)
    held = {}
    for bit in reversed(range(1, bits_of(parts))):
        first = swap(halves[0], "dp", 1 << bit)
        first, second = lax.optimization_barrier((first, halves[1]))
        held[1 << bit] = [first, swap(second, "dp", 1 << bit)]
        for mask in [m for m in held if m >> (bit + 1)]:
            held[mask | (1 << bit)] = [swap(h, "dp", 1 << bit) for h in held[mask]]
    if parts > 1:
        far = list(held)
        held[1] = [swap(own_keys, "dp", 1)]
    held[0] = [own_keys]
    other = swap(mine, "dp", parts)
    step = jnp.zeros((8, CLUSTER), jnp.float32)
    for _ in range(1):
        step, _ = lax.optimization_barrier((step, other))
        step = swap(step, "tensor", 1)
    other, _ = lax.optimization_barrier((other, step))

    def table(asked):
        asked = asked.reshape(requests)
        owner, local = asked // clusters, asked % clusters
        earlier = jnp.arange(requests)[None, :] < jnp.arange(requests)[:, None]
        same = owner[:, None] == owner[None, :]
        place = (owner ^ here) * cap + jnp.sum(jnp.where(same & earlier, 1, 0), axis=1)
        code = VALID + jnp.arange(requests) // PARTNERS * 256 + local
        slots = jnp.arange(parts * cap)[:, None] == place[None, :]
        return jnp.sum(jnp.where(slots, code[None, :], 0), axis=1).astype(jnp.int32)

    tab = (table(matching), table(swap(matching, "dp", parts)))

    unit = 2 * CLUSTER * CLUSTER * width
    rows = {0: mine, 1: other}
    chunks, waits = [], (tab[1],)
    for n, (groups, count) in enumerate(plans):
        if n == 1 and parts > 1:
            for mask in far:
                last, _ = lax.optimization_barrier((held[mask][-1], waits[0]))
                held[mask | 1] = [swap(h, "dp", 1) for h in held[mask][:-1] + [last]]
        masks = sorted({m for m, _, _ in groups})
        askers = sorted({r for _, r, _ in groups})
        splits = tuple((m, len(held[m])) for m in masks)
        half = jax.ShapeDtypeStruct((ways // 2, count, share, CLUSTER), f32)
        keep, give, done = call(
            f"logits_{n}",
            functools.partial(logits_kernel, groups, splits, clusters, cap, ways),
            (half, half, jax.ShapeDtypeStruct((8, CLUSTER), f32)),
            [], count * unit,
            (tab[0], tab[max(askers)], rank, *[rows[r] for r in askers],
             *[k for m in masks for k in held[m]]),
            3, waits,
        )
        waits = (done,)
        got = swap(give, "tensor", 1)
        bit = 1
        while (1 << bit) < ways:
            keep = keep + got
            pairs = keep.reshape((keep.shape[0] // 2, 2) + keep.shape[1:])
            keep = pairs[:, 0]
            got = swap(pairs[:, 1], "tensor", 1 << bit)
            bit += 1
        chunks.append((keep + got)[0])
        waits += (chunks[0],) if len(chunks) == 1 else ()

    tile = jax.ShapeDtypeStruct((share, CLUSTER), f32)
    levels = pltpu.VMEM((2 * clusters + 1, share, CLUSTER), f32)
    stats = call(
        "row_stats",
        functools.partial(stats_kernel, plans, clusters, cap, scale),
        tile, [levels, levels], 0, (*tab, *chunks), 2,
    )
    facing = swap(stats, "dp", parts)
    *weights, loss_rows = call(
        "weights",
        functools.partial(weights_kernel, plans, clusters, cap, scale),
        [jax.ShapeDtypeStruct(chunks[n].shape, bf16) for n in range(len(plans))] + [tile],
        [levels], 0, (*tab, rank, stats, facing, *chunks), 3,
    )
    order = [0]
    for bit in reversed(range(bits_of(ways))):
        order += [at | (1 << bit) for at in order]
    pieces = [None] * len(plans)
    for n in reversed(range(len(plans))):
        pieces[n] = [weights[n]]
        for bit in reversed(range(bits_of(ways))):
            pieces[n] += [swap(piece, "tensor", 1 << bit) for piece in pieces[n]]

    def chosen(wanted):
        groups = [
            (n, m, r, first)
            for n, (plan, _) in enumerate(plans)
            for m, r, first in plan
            if wanted(m, r)
        ]
        used = sorted({g[0] for g in groups})
        groups = tuple((used.index(n), m, r, first) for n, m, r, first in groups)
        return groups, len(used), [p for n in used for p in pieces[n]]

    def gradients(name, wanted, waits=()):
        found, used, args = chosen(
            lambda m, r: any(w[1] == (m if w[0] == "term" else r) for w in wanted)
        )
        asked = sorted({g[1] for g in found}) if any(w[0] == "query" for w in wanted) else []
        tasks, shapes, came = [], [], []
        for w in wanted:
            groups = tuple(g for g in found if w[1] == (g[1] if w[0] == "term" else g[2]))
            lo, wides, add = w[2:] if w[0] == "term" else (0, (width,), [])
            kept = bf16 if w[1] else f32
            tasks.append((w[0], groups, lo, len(add), len(wides)))
            shapes += [jax.ShapeDtypeStruct(cube[:2] + (wide,), kept) for wide in wides]
            came += add
        splits = tuple((m, len(held[m])) for m in asked)
        return call(
            name,
            functools.partial(grad_kernel, tasks, used, splits, clusters, cap, order),
            shapes, [pltpu.VMEM(cube, f32)], unit * cap * len(tasks),
            (*tab, rank, mine, other, *[k for m in asked for k in held[m]], *args, *came),
            3, waits,
        )

    def lowest(m):
        return bits_of(m & -m) if m else bits_of(parts)

    cut = max(1, width * OUT_CUT // 8 // CLUSTER) * CLUSTER
    halves = ((0, cut), (cut, width - cut))
    odd = range(3, parts, 2)
    terms, waits = {}, ()
    if odd:
        made = gradients("terms_far", [("term", m, 0, (cut, width - cut), []) for m in odd], (pieces[1][1],))
        terms = {m: made[2 * i : 2 * i + 2] for i, m in enumerate(odd)}
        waits = (made[0],)
    lead = [("query", 1)] + ([("term", 1, 0, (width,), [])] if parts > 1 else [])
    far_q, *near = gradients("grads_lead", lead, waits)
    own_p, own_q = gradients("grads_own", [("term", 0, 0, (width,), []), ("query", 0)], (far_q,))
    came = []
    for m in sorted(range(2, parts, 2), key=lambda m: (lowest(m), -m)):
        came = [[swap(t, "dp", 1 << b) for t in terms[m | (1 << b)]] for b in range(lowest(m))]
        terms[m] = []
        for i, (lo, wide) in enumerate(halves):
            add = [got[i] for got in came]
            terms[m] += gradients(f"term_{m}_{i}", [("term", m, lo, (wide,), add)])
    if near:
        if came:
            near = [lax.optimization_barrier((near[0], came[0][-1]))[0]]
        terms[1] = near
    came = [swap(t, "dp", 1 << b) for b in range(bits_of(parts)) for t in terms[1 << b]]
    far_q = swap(far_q, "dp", parts)
    zero = jnp.zeros((8, CLUSTER), f32)
    grad_q, squares = summed(zero, own_q, far_q)
    grad_p, squares = summed(squares, own_p, *came)

    sums = jnp.stack([jnp.sum(loss_rows.reshape(-1, 8, CLUSTER), axis=0), squares])
    for bit in range(bits_of(ways)):
        sums = sums + swap(sums, "tensor", 1 << bit)
    for bit in range(bits_of(size)):
        sums = sums + swap(sums, "dp", 1 << bit)
    sums = jnp.sum(sums, axis=(1, 2))
    all_rows = clusters * CLUSTER * size
    clip_limit = 0.25 * jnp.sqrt(jnp.float32(2 * all_rows * width * ways))
    factor = jnp.minimum(jnp.float32(1.0), clip_limit / jnp.sqrt(sums[1] + 1e-06))
    flat = queries.shape
    grad_queries = (grad_q * factor).astype(bf16).reshape(flat)
    grad_passages = (grad_p * factor).astype(bf16).reshape(flat)
    return (grad_queries, grad_passages, sums[0] / all_rows)


def solution(mesh):
    in_specs = (P("dp", "tensor"), P("dp", "tensor"), P("dp", None))
    out_specs = (P("dp", "tensor"), P("dp", "tensor"), P())
    return jax.shard_map(shards, mesh=mesh, in_specs=in_specs, out_specs=out_specs, check_vma=False)
```

```python
import functools

import jax
import jax.numpy as jnp
from jax import lax
from jax.experimental import pallas as pl
from jax.experimental.pallas import tpu as pltpu
from jax.sharding import PartitionSpec as P

CLUSTER = 128
PARTNERS = 8
LOW = -3.0e38
VALID = 1 << 16
VMEM_LIMIT = 56 * 1024 * 1024
SLACK = 4 * 1024 * 1024
COST = 1
IN_CUT = 4
OUT_CUT = 4

VM = pl.BlockSpec(memory_space=pltpu.VMEM)
SM = pl.BlockSpec(memory_space=pltpu.SMEM)
ANY = pl.BlockSpec(memory_space=pl.ANY)
NT = (((1,), (1,)), ((), ()))
TN = (((0,), (0,)), ((), ()))
NN = (((1,), (0,)), ((), ()))


def bits_of(size):
    return size.bit_length() - 1


def swap(value, axis, mask):
    size = lax.axis_size(axis)
    return lax.ppermute(value, axis, [(i, i ^ mask) for i in range(size)])


def size_of(shape):
    return shape.size * shape.dtype.itemsize


def call(name, kernel, out_shape, scratch, flops, args, smem, waits=()):
    outs = jax.tree.leaves(out_shape)
    moved = sum(size_of(a) for a in args[smem:]) + sum(size_of(o) for o in outs)
    held = moved + sum(size_of(jax.ShapeDtypeStruct(x.shape, x.dtype)) for x in scratch)

    def body(*refs):
        kernel(*refs[: len(args)], *refs[len(args) + len(waits) :])

    return pl.pallas_call(
        body,
        name=name,
        out_shape=out_shape,
        in_specs=[SM] * smem + [VM] * (len(args) - smem) + [ANY] * len(waits),
        out_specs=jax.tree.map(lambda _: VM, out_shape),
        scratch_shapes=scratch,
        compiler_params=pltpu.CompilerParams(vmem_limit_bytes=min(held + SLACK, VMEM_LIMIT)),
        cost_estimate=pl.CostEstimate(flops=flops // COST, bytes_accessed=moved // COST, transcendentals=0),
    )(*args, *waits)


def unpack(code):
    return code >= VALID, (code >> 8) & 255, code & 255


def layout(parts, clusters, cap):
    plans = [
        [(m, 0) for m in range(min(parts, 2))],
        [(m, 1) for m in range(min(parts, 2))] + [(2, r) for r in (0, 1) if parts > 2],
        [(m, r) for m in range(3, parts) for r in (0, 1)],
    ]
    chunks = []
    for plan in plans:
        groups, first = [], clusters if (0, 0) in plan else 0
        for mask, requester in plan:
            groups.append((mask, requester, first))
            first += cap
        if groups:
            chunks.append((tuple(groups), first))
    return tuple(chunks)


def columns(refs):
    start = 0
    for ref in refs:
        yield ref, slice(start, start + ref.shape[-1])
        start += ref.shape[-1]


def share_rows(me, at, share):
    return pl.ds(pl.multiple_of((me ^ at) * share, share), share)


def rows_of(ref, c, me, ways, cut=slice(None)):
    share = CLUSTER // ways
    blocks = [ref[c, share_rows(me, at, share), cut] for at in range(ways)]
    return jnp.concatenate(blocks, axis=0)


def logits_kernel(groups, splits, clusters, cap, ways, tab_a, tab_b, rank, *refs):
    tab = (tab_a, tab_b)
    share = CLUSTER // ways
    me = rank[0]
    askers = sorted({r for _, r, _ in groups})
    rows = dict(zip(askers, refs))
    at_ref, keys = len(askers), {}
    for m, split in splits:
        keys[m] = refs[at_ref : at_ref + split]
        at_ref += split
    low, high, done = refs[at_ref:]
    done[...] = jnp.zeros_like(done)

    def one(row_ref, c, mask, e, slot):
        row = rows_of(row_ref, c, me, ways)
        block = None
        for key, at in columns(keys[mask]):
            part = lax.dot_general(row[:, at], key[e], NT, preferred_element_type=jnp.float32)
            block = part if block is None else block + part
        for at in range(ways):
            (high if at % 2 else low)[at // 2, slot] = block[at * share : (at + 1) * share]

    if any(first and (mask, r) == (0, 0) for mask, r, first in groups):

        @pl.loop(0, clusters)
        def _(c):
            one(rows[0], c, 0, c, c)

    @pl.loop(0, cap)
    def _(j):
        for mask, requester, first in groups:
            _, c, e = unpack(tab[requester][mask * cap + j])
            one(rows[requester], c, mask, e, first + j)


def each_slot(visit, chunks, plans, clusters, cap, tab):
    for n, (groups, _) in enumerate(plans):
        if any(first and (mask, r) == (0, 0) for mask, r, first in groups):
            for c in range(clusters):
                visit(n, chunks[n], c, c, None)

        @pl.loop(0, cap)
        def _(j):
            for mask, requester, first in groups:
                ok, c, _ = unpack(tab[requester][mask * cap + j])
                at = jnp.where(ok, requester * clusters + c, 2 * clusters)
                visit(n, chunks[n], first + j, at, ok)


def stats_kernel(plans, clusters, cap, scale, tab_a, tab_b, *refs):
    tab = (tab_a, tab_b)
    parts = len(plans)
    chunks, stats, top, total = refs[:parts], refs[parts], refs[parts + 1], refs[parts + 2]
    top[...] = jnp.full_like(top, LOW)
    total[...] = jnp.zeros_like(total)

    def raise_top(n, ref, slot, at, ok):
        top[at] = jnp.maximum(top[at], ref[slot] * scale)

    each_slot(raise_top, chunks, plans, clusters, cap, tab)
    for c in range(2 * clusters + 1):
        top[c] = jnp.broadcast_to(jnp.max(top[c], axis=-1, keepdims=True), top.shape[1:])

    def add_total(n, ref, slot, at, ok):
        total[at] = total[at] + jnp.exp(ref[slot] * scale - top[at])

    each_slot(add_total, chunks, plans, clusters, cap, tab)
    lane = lax.broadcasted_iota(jnp.int32, stats.shape, 1)
    out = jnp.zeros(stats.shape, jnp.float32)
    for c in range(2 * clusters):
        out = jnp.where(lane == c, top[c], out)
        sums = jnp.sum(total[c], axis=-1, keepdims=True)
        out = jnp.where(lane == 2 * clusters + c, sums, out)
    stats[...] = out


def weights_kernel(plans, clusters, cap, scale, tab_a, tab_b, rank, here, there, *refs):
    tab = (tab_a, tab_b)
    parts = len(plans)
    chunks, outs = refs[:parts], refs[parts : 2 * parts]
    loss, level = refs[2 * parts :]
    shape = here.shape
    row = lax.broadcasted_iota(jnp.int32, shape, 0) + rank[0] * shape[0]
    lane = lax.broadcasted_iota(jnp.int32, shape, 1)
    target = (row == lane).astype(jnp.float32)
    k = 2 * clusters
    for c in range(k):
        p = (c + clusters) % k
        top_a, top_b = here[:, c : c + 1], there[:, p : p + 1]
        sum_a, sum_b = here[:, k + c : k + c + 1], there[:, k + p : k + p + 1]
        top = jnp.maximum(top_a, top_b)
        total = sum_a * jnp.exp(top_a - top) + sum_b * jnp.exp(top_b - top)
        level[c] = jnp.broadcast_to(top + jnp.log(total), shape)
    level[k] = jnp.zeros(shape, jnp.float32)
    loss[...] = jnp.zeros(shape, jnp.float32)

    def weigh(n, ref, slot, at, ok):
        logits = ref[slot] * scale
        chances = jnp.exp(logits - level[at])
        if ok is None:
            chances = chances - target
            loss[...] += jnp.where(lane == 0, level[at], 0.0) - logits * target
        else:
            chances = jnp.where(ok, chances, 0.0)
        outs[n][slot] = chances.astype(jnp.bfloat16)

    each_slot(weigh, chunks, plans, clusters, cap, tab)


def whole_weights(pieces, order, slot):
    by_distance = sorted(zip(order, pieces), key=lambda pair: pair[0])
    return jnp.concatenate([piece[slot] for _, piece in by_distance], axis=0)


def take_pieces(refs, count, ways):
    return [refs[i * ways : (i + 1) * ways] for i in range(count)], refs[count * ways :]


def grad_kernel(tasks, used, splits, clusters, cap, order, tab_a, tab_b, rank, *refs):
    tab, ways, me = (tab_a, tab_b), len(order), rank[0]
    share = CLUSTER // ways
    mine, other = refs[:2]
    keys, at_ref = {}, 2
    for m, split in splits:
        keys[m] = refs[at_ref : at_ref + split]
        at_ref += split
    pieces, refs = take_pieces(refs[at_ref:], used, ways)
    total = refs[-1]
    come_at, out_at = 0, sum(task[3] for task in tasks)
    for kind, groups, lo, arrived, outputs in tasks:
        came = refs[come_at : come_at + arrived]
        outs = refs[out_at : out_at + outputs]
        come_at, out_at = come_at + arrived, out_at + outputs
        span = sum(out.shape[-1] for out in outs)

        def term(n, requester, slot, mask, c, e, fresh):
            w = whole_weights(pieces[n], order, slot)
            row = rows_of(other if requester else mine, c, me, ways, slice(lo, lo + span))
            part = lax.dot_general(w, row, TN, preferred_element_type=jnp.float32)
            total[e, :, :span] = part if fresh else total[e, :, :span] + part

        def query(n, requester, slot, mask, c, e, fresh):
            w = whole_weights(pieces[n], order, slot)
            for key, at in columns(keys[mask]):
                part = lax.dot_general(w, key[e], NN, preferred_element_type=jnp.float32)
                total[c, :, at] = part if fresh else total[c, :, at] + part

        visit = term if kind == "term" else query
        own = [g for g in groups if g[1:3] == (0, 0) and g[3]]
        if own:

            @pl.loop(0, clusters)
            def _(c):
                visit(own[0][0], 0, c, 0, c, c, True)

        else:
            total[:, :, :span] = jnp.zeros(total.shape[:2] + (span,), jnp.float32)

        @pl.loop(0, cap)
        def _(j):
            for n, mask, requester, first in groups:
                _, c, e = unpack(tab[requester][mask * cap + j])
                visit(n, requester, first + j, mask, c, e, False)

        @pl.loop(0, clusters)
        def _(c):
            for out, at in columns(outs):
                value = total[c, :, at]
                for ref in came:
                    value = value + ref[c].astype(jnp.float32)
                if kind == "term":
                    out[c] = value.astype(out.dtype)
                else:
                    for at in range(ways):
                        block = value[at * share : (at + 1) * share]
                        out[c, share_rows(me, at, share), :] = block.astype(out.dtype)


def sum_kernel(before, base, *refs):
    parts, (out, squares) = refs[:-2], refs[-2:]
    squares[...] = before[...]

    @pl.loop(0, out.shape[0])
    def _(c):
        value = base[c]
        for ref in parts:
            if ref.shape == base.shape:
                value = value + ref[c].astype(jnp.float32)
        sides = [ref for ref in parts if ref.shape != base.shape]
        for i in range(0, len(sides), 2):
            pair = [ref[c].astype(jnp.float32) for ref in sides[i : i + 2]]
            value = value + jnp.concatenate(pair, axis=-1)
        out[c] = value
        square = jnp.sum((value * value).reshape(-1, 8, value.shape[-1]), axis=0)
        lanes = [square[:, i : i + CLUSTER] for i in range(0, value.shape[-1], CLUSTER)]
        squares[...] += sum(lanes)


def summed(before, base, *parts):
    shapes = tuple(jax.ShapeDtypeStruct(a.shape, a.dtype) for a in (base, before))
    return call("summed", sum_kernel, shapes, [], 0, (before, base, *parts), 0)


def split_of(mask):
    return 2 if mask > 1 else 1


def shards(queries, passages, matching):
    bf16, f32 = jnp.bfloat16, jnp.float32
    size, ways = lax.axis_size("dp"), lax.axis_size("tensor")
    clusters, width = matching.shape[0], queries.shape[1]
    requests = clusters * PARTNERS
    cap = -(-requests // size)
    parts = size // 2
    share = CLUSTER // ways
    scale = (width * ways) ** (-0.5)
    cube = (clusters, CLUSTER, width)
    mine, own_keys = queries.reshape(cube), passages.reshape(cube)
    here = lax.axis_index("dp").astype(jnp.int32)
    rank = lax.axis_index("tensor").astype(jnp.int32).reshape(1)
    plans = layout(parts, clusters, cap)

    cut = max(1, width * IN_CUT // 8 // CLUSTER) * CLUSTER
    halves = jnp.split(own_keys, [cut], axis=-1)
    held = {}
    for bit in reversed(range(1, bits_of(parts))):
        first = swap(halves[0], "dp", 1 << bit)
        first, second = lax.optimization_barrier((first, halves[1]))
        held[1 << bit] = [first, swap(second, "dp", 1 << bit)]
        for mask in [m for m in held if m >> (bit + 1)]:
            held[mask | (1 << bit)] = [swap(h, "dp", 1 << bit) for h in held[mask]]
    if parts > 1:
        far = list(held)
        held[1] = [swap(own_keys, "dp", 1)]
    held[0] = [own_keys]
    other = swap(mine, "dp", parts)
    step = jnp.zeros((8, CLUSTER), jnp.float32)
    for _ in range(1):
        step, _ = lax.optimization_barrier((step, other))
        step = swap(step, "tensor", 1)
    other, _ = lax.optimization_barrier((other, step))

    def table(asked):
        asked = asked.reshape(requests)
        owner, local = asked // clusters, asked % clusters
        earlier = jnp.arange(requests)[None, :] < jnp.arange(requests)[:, None]
        same = owner[:, None] == owner[None, :]
        place = (owner ^ here) * cap + jnp.sum(jnp.where(same & earlier, 1, 0), axis=1)
        code = VALID + jnp.arange(requests) // PARTNERS * 256 + local
        slots = jnp.arange(parts * cap)[:, None] == place[None, :]
        return jnp.sum(jnp.where(slots, code[None, :], 0), axis=1).astype(jnp.int32)

    tab = (table(matching), table(swap(matching, "dp", parts)))

    unit = 2 * CLUSTER * CLUSTER * width
    rows = {0: mine, 1: other}
    chunks, waits = [], (tab[1],)
    for n, (groups, count) in enumerate(plans):
        if n == 1 and parts > 1:
            for mask in far:
                last, _ = lax.optimization_barrier((held[mask][-1], waits[0]))
                held[mask | 1] = [swap(h, "dp", 1) for h in held[mask][:-1] + [last]]
        masks = sorted({m for m, _, _ in groups})
        askers = sorted({r for _, r, _ in groups})
        splits = tuple((m, len(held[m])) for m in masks)
        half = jax.ShapeDtypeStruct((ways // 2, count, share, CLUSTER), f32)
        keep, give, done = call(
            f"logits_{n}",
            functools.partial(logits_kernel, groups, splits, clusters, cap, ways),
            (half, half, jax.ShapeDtypeStruct((8, CLUSTER), f32)),
            [], count * unit,
            (tab[0], tab[max(askers)], rank, *[rows[r] for r in askers],
             *[k for m in masks for k in held[m]]),
            3, waits,
        )
        waits = (done,)
        got = swap(give, "tensor", 1)
        bit = 1
        while (1 << bit) < ways:
            keep = keep + got
            pairs = keep.reshape((keep.shape[0] // 2, 2) + keep.shape[1:])
            keep = pairs[:, 0]
            got = swap(pairs[:, 1], "tensor", 1 << bit)
            bit += 1
        chunks.append((keep + got)[0])
        waits += (chunks[0],) if len(chunks) == 1 else ()

    tile = jax.ShapeDtypeStruct((share, CLUSTER), f32)
    levels = pltpu.VMEM((2 * clusters + 1, share, CLUSTER), f32)
    stats = call(
        "row_stats",
        functools.partial(stats_kernel, plans, clusters, cap, scale),
        tile, [levels, levels], 0, (*tab, *chunks), 2,
    )
    facing = swap(stats, "dp", parts)
    *weights, loss_rows = call(
        "weights",
        functools.partial(weights_kernel, plans, clusters, cap, scale),
        [jax.ShapeDtypeStruct(chunks[n].shape, bf16) for n in range(len(plans))] + [tile],
        [levels], 0, (*tab, rank, stats, facing, *chunks), 3,
    )
    order = [0]
    for bit in reversed(range(bits_of(ways))):
        order += [at | (1 << bit) for at in order]
    pieces = [None] * len(plans)
    for n in reversed(range(len(plans))):
        pieces[n] = [weights[n]]
        for bit in reversed(range(bits_of(ways))):
            pieces[n] += [swap(piece, "tensor", 1 << bit) for piece in pieces[n]]

    def chosen(wanted):
        groups = [
            (n, m, r, first)
            for n, (plan, _) in enumerate(plans)
            for m, r, first in plan
            if wanted(m, r)
        ]
        used = sorted({g[0] for g in groups})
        groups = tuple((used.index(n), m, r, first) for n, m, r, first in groups)
        return groups, len(used), [p for n in used for p in pieces[n]]

    def gradients(name, wanted, waits=()):
        found, used, args = chosen(
            lambda m, r: any(w[1] == (m if w[0] == "term" else r) for w in wanted)
        )
        asked = sorted({g[1] for g in found}) if any(w[0] == "query" for w in wanted) else []
        tasks, shapes, came = [], [], []
        for w in wanted:
            groups = tuple(g for g in found if w[1] == (g[1] if w[0] == "term" else g[2]))
            lo, wides, add = w[2:] if w[0] == "term" else (0, (width,), [])
            kept = bf16 if w[1] else f32
            tasks.append((w[0], groups, lo, len(add), len(wides)))
            shapes += [jax.ShapeDtypeStruct(cube[:2] + (wide,), kept) for wide in wides]
            came += add
        splits = tuple((m, len(held[m])) for m in asked)
        return call(
            name,
            functools.partial(grad_kernel, tasks, used, splits, clusters, cap, order),
            shapes, [pltpu.VMEM(cube, f32)], unit * cap * len(tasks),
            (*tab, rank, mine, other, *[k for m in asked for k in held[m]], *args, *came),
            3, waits,
        )

    def lowest(m):
        return bits_of(m & -m) if m else bits_of(parts)

    cut = max(1, width * OUT_CUT // 8 // CLUSTER) * CLUSTER
    halves = ((0, cut), (cut, width - cut))
    odd = range(3, parts, 2)
    terms, waits = {}, ()
    if odd:
        made = gradients("terms_far", [("term", m, 0, (cut, width - cut), []) for m in odd], (pieces[1][1],))
        terms = {m: made[2 * i : 2 * i + 2] for i, m in enumerate(odd)}
        waits = (made[0],)
    lead = [("query", 1)] + ([("term", 1, 0, (width,), [])] if parts > 1 else [])
    far_q, *near = gradients("grads_lead", lead, waits)
    own_p, own_q = gradients("grads_own", [("term", 0, 0, (width,), []), ("query", 0)], (far_q,))
    came = []
    for m in sorted(range(2, parts, 2), key=lambda m: (lowest(m), -m)):
        came = [[swap(t, "dp", 1 << b) for t in terms[m | (1 << b)]] for b in range(lowest(m))]
        terms[m] = []
        for i, (lo, wide) in enumerate(halves):
            add = [got[i] for got in came]
            terms[m] += gradients(f"term_{m}_{i}", [("term", m, lo, (wide,), add)])
    if near:
        if came:
            near = [lax.optimization_barrier((near[0], came[0][-1]))[0]]
        terms[1] = near
    came = [swap(t, "dp", 1 << b) for b in range(bits_of(parts)) for t in terms[1 << b]]
    far_q = swap(far_q, "dp", parts)
    zero = jnp.zeros((8, CLUSTER), f32)
    grad_q, squares = summed(zero, own_q, far_q)
    grad_p, squares = summed(squares, own_p, *came)

    sums = jnp.stack([jnp.sum(loss_rows.reshape(-1, 8, CLUSTER), axis=0), squares])
    for bit in range(bits_of(ways)):
        sums = sums + swap(sums, "tensor", 1 << bit)
    for bit in range(bits_of(size)):
        sums = sums + swap(sums, "dp", 1 << bit)
    sums = jnp.sum(sums, axis=(1, 2))
    all_rows = clusters * CLUSTER * size
    clip_limit = 0.25 * jnp.sqrt(jnp.float32(2 * all_rows * width * ways))
    factor = jnp.minimum(jnp.float32(1.0), clip_limit / jnp.sqrt(sums[1] + 1e-06))
    flat = queries.shape
    grad_queries = (grad_q * factor).astype(bf16).reshape(flat)
    grad_passages = (grad_p * factor).astype(bf16).reshape(flat)
    return (grad_queries, grad_passages, sums[0] / all_rows)


def solution(mesh):
    in_specs = (P("dp", "tensor"), P("dp", "tensor"), P("dp", None))
    out_specs = (P("dp", "tensor"), P("dp", "tensor"), P())
    return jax.shard_map(shards, mesh=mesh, in_specs=in_specs, out_specs=out_specs, check_vma=False)
```
